256 devices in a mesh: span: 16 (over x, y_hi, core), tok: 16 (over z, y_lo).
Axes of the slice: x: 4, y: 4 (y_hi: 2, y_lo: 2; y = y_hi * 2 + y_lo), z: 8, core: 2. Of those that a mesh axis runs over, the one named last changes fastest.
Arguments:
- tokens: bfloat16 [131072, 256], P(('span', 'tok')), may hold values from -6 to 6
- w_in: bfloat16 [256, 768], replicated, may hold values from -0.375 to 0.375
- short_filter: float32 [3, 768], replicated, may hold values from -3 to 3
- long_filter: bfloat16 [256, 8192], P('tok'), may hold values from -0.0625 to 0.0625
- skip_gain: float32 [256], P('tok'), may hold values from 0.5 to 1.5
- w_out: bfloat16 [256, 256], replicated, may hold values from -0.375 to 0.375
Outputs:
- output: bfloat16 [131072, 256], P(('span', 'tok'))
The draws below stay inside these ranges and needn't reach their ends.
All inputs are finite; a program needn't handle non-finite values.
Results may differ from the reference program's by a relative error of at most 0.0081.
Values may be sent and summed in bfloat16 or wider, within the bound.
No kernel may reach another device: no remote copies, remote signals or barrier semaphores. Data moves between devices by JAX's collectives and lax.ppermute only.
A program may use at most 64 MiB of HBM per device.

```python
import jax
import jax.numpy as jnp
from jax import lax

D = 256
FILT = 8192
SEQ = 131072


def shard_levels(own_key, extent, pieces, least, top_value):
    gain = 1.0
    for axis_at, blocks in pieces:
        heights = jax.random.uniform(jax.random.fold_in(jax.random.fold_in(own_key, 6), axis_at), (blocks,), jnp.float32, least / len(pieces), top_value / len(pieces))
        gain = gain * jnp.repeat(jnp.exp(heights), extent[axis_at] // blocks).reshape((-1,) + (1,) * (len(extent) - 1 - axis_at))
    return gain


def scatter_about(stream_key, dims, width, most, split=(), dtype=jnp.bfloat16):
    level = shard_levels(stream_key, dims, split, -0.22, 0.18) if split else 1.0
    drawn = jax.random.normal(stream_key, dims, jnp.float32) * width * level
    return jnp.minimum(jnp.maximum(drawn, -most), most).astype(dtype)


def setup_inputs(seed: int = 0) -> dict:
    arg_keys = jax.random.split(jax.random.key(seed), 7)
    tokens = scatter_about(arg_keys[0], (SEQ, D), 1.0, 6.0, ((0, 256),))
    w_in = scatter_about(arg_keys[1], (D, 3 * D), D ** -0.5, 0.375)
    short_filter = scatter_about(arg_keys[2], (3, 3 * D), 0.6, 3.0, (), jnp.float32)
    long_filter = scatter_about(arg_keys[3], (D, FILT), FILT ** -0.5, 0.0625, ((0, 16),))
    skip_gain = jnp.clip(0.5 + 1.0 * jax.random.uniform(arg_keys[4], (D,), jnp.float32) ** shard_levels(arg_keys[4], (D,), ((0, 16),), -0.2, 0.2), 0.5, 1.5)
    w_out = scatter_about(arg_keys[5], (D, D), D ** -0.5, 0.375)
    return {"tokens": tokens, "w_in": w_in, "short_filter": short_filter, "long_filter": long_filter, "skip_gain": skip_gain, "w_out": w_out}


def reference(tokens, w_in, short_filter, long_filter, skip_gain, w_out):
    projected = jnp.dot(tokens, w_in, preferred_element_type=jnp.float32).astype(jnp.bfloat16)
    projected = lax.optimization_barrier(projected).astype(jnp.float32)
    padded = jnp.pad(projected, ((2, 0), (0, 0)))
    mixed = short_filter[0] * padded[2:] + short_filter[1] * padded[1:-1] + short_filter[2] * padded[:-2]
    query_rows = mixed[:, :D]
    key_rows = mixed[:, D:2 * D]
    value_rows = mixed[:, 2 * D:]
    product = (key_rows * value_rows).astype(jnp.bfloat16)
    total = product.shape[0]
    taps_count = long_filter.shape[1]
    fft_len = 1
    while fft_len < total + taps_count:
        fft_len = fft_len * 2
    product_f = lax.optimization_barrier(product).astype(jnp.float32)
    spectrum = jnp.fft.rfft(product_f, n=fft_len, axis=0) * jnp.fft.rfft(long_filter.astype(jnp.float32).T, n=fft_len, axis=0)
    conv_full = jnp.fft.irfft(spectrum, n=fft_len, axis=0)[:total].astype(jnp.float32)
    convolved = (conv_full + skip_gain * product_f).astype(jnp.bfloat16)
    convolved = lax.optimization_barrier(convolved).astype(jnp.float32)
    gated = (query_rows * convolved).astype(jnp.bfloat16)
    return jnp.dot(gated, w_out, preferred_element_type=jnp.float32).astype(jnp.bfloat16)
```

```python
import jax
import jax.numpy as jnp
import numpy as np
from jax import lax
from jax.experimental import pallas as pl
from jax.experimental.pallas import tpu as pltpu
from jax.sharding import PartitionSpec as P

D = 256
LANES = 128
HALF = 64
RIM = 16
POINTS = LANES * LANES


def dft_tables():
    ka = np.arange(HALF) + 0.5
    idx = np.arange(LANES)
    wave = lambda phase: np.exp(-2j * np.pi * phase)
    rows = wave(np.outer(ka, idx) / LANES)
    twist = wave(np.outer(ka, idx) / POINTS)
    cols = wave(np.outer(idx, idx) / LANES)
    into = np.concatenate([rows.real, rows.imag], 0)
    back = into.T[HALF:] * (2.0 / POINTS)
    cols_in = np.block([[cols.real, cols.imag], [-cols.imag, cols.real]])
    cols_out = np.block([[cols.real.T, -cols.imag.T], [cols.imag.T, cols.real.T]])
    bf = lambda a: jnp.asarray(a.astype(np.float32)).astype(jnp.bfloat16)
    twist = np.stack([twist.real, twist.imag]).astype(np.float32)
    return bf(into), bf(cols_in), bf(cols_out), bf(back), jnp.asarray(twist)


def dot(a, b):
    return jnp.dot(a, b, preferred_element_type=jnp.float32)


def project_kernel(tokens_ref, rim_ref, w_ref, taps_ref, product_ref, query_ref):
    rows = tokens_ref.shape[0]
    taps = taps_ref[...]

    def mixed(part):
        cols = slice(part * D, (part + 1) * D)
        weights = w_ref[:, cols]
        body = dot(tokens_ref[...], weights)
        head = dot(rim_ref[...], weights)
        both = jnp.concatenate([head, body], axis=0)
        both = both.astype(jnp.bfloat16).astype(jnp.float32)
        one = pltpu.roll(both, 1, axis=0)
        two = pltpu.roll(both, 2, axis=0)
        out = taps[0:1, cols] * both + taps[1:2, cols] * one + taps[2:3, cols] * two
        return out[RIM:]

    query_ref[...] = mixed(0)
    product = mixed(1) * mixed(2)
    product_ref[...] = jnp.transpose(product, (1, 0)).astype(jnp.bfloat16)


def project(tokens, rim, w_in, short_filter):
    rows = tokens.shape[0]
    return pl.pallas_call(
        project_kernel,
        out_shape=(
            jax.ShapeDtypeStruct((D, rows), jnp.bfloat16),
            jax.ShapeDtypeStruct((rows, D), jnp.float32),
        ),
        compiler_params=pltpu.CompilerParams(vmem_limit_bytes=24 << 20),
        cost_estimate=pl.CostEstimate(
            flops=2 * rows * D * 3 * D, bytes_accessed=2 << 20, transcendentals=0
        ),
        name="project",
    )(tokens, rim, w_in, short_filter)


def put_rows(load, scratch, chans, tiles, at):
    for tile in range(tiles):
        scratch[pl.ds((at + tile) * chans, chans), :] = load(tile).astype(jnp.float32)


def by_channel(scratch, chans, at, tiles):
    return jnp.concatenate(
        [scratch[pl.ds(at * chans + c, tiles, stride=chans), :] for c in range(chans)], axis=1
    )


def forward(into, cols_in, twist_re, twist_im, data, chans):
    first = dot(into, data)
    spun = []
    for c in range(chans):
        re = first[:HALF, c * LANES : (c + 1) * LANES]
        im = first[HALF:, c * LANES : (c + 1) * LANES]
        spun.append(
            jnp.concatenate(
                [re * twist_re - im * twist_im, re * twist_im + im * twist_re], axis=1
            ).astype(jnp.bfloat16)
        )
    return dot(jnp.concatenate(spun, axis=0), cols_in)


def spectrum_kernel(filter_ref, into_ref, cols_in_ref, twist_ref, out_ref, rows_ref):
    chans, taps = filter_ref.shape
    tiles = taps // LANES
    put_rows(lambda i: filter_ref[:, i * LANES : (i + 1) * LANES], rows_ref, chans, tiles, 0)
    data = by_channel(rows_ref, chans, 0, tiles).astype(jnp.bfloat16)
    out_ref[...] = forward(
        into_ref[:, :tiles], cols_in_ref[...], twist_ref[0], twist_ref[1], data, chans
    )


def spectrum(long_filter, into, cols_in, twist):
    chans, taps = long_filter.shape
    return pl.pallas_call(
        spectrum_kernel,
        out_shape=jax.ShapeDtypeStruct((chans * HALF, 2 * LANES), jnp.float32),
        scratch_shapes=[pltpu.VMEM((taps // LANES * chans, LANES), jnp.float32)],
        compiler_params=pltpu.CompilerParams(vmem_limit_bytes=24 << 20),
        cost_estimate=pl.CostEstimate(
            flops=400_000_000, bytes_accessed=3 << 20, transcendentals=0
        ),
        name="spectrum",
    )(long_filter, into, cols_in, twist)


def convolve_kernel(
    past_ref, own_ref, spec_ref, gain_ref, into_ref, cols_in_ref, cols_out_ref, back_ref,
    twist_ref, out_ref, rows_ref,
):
    peers, chans, width = own_ref.shape
    per = width // LANES
    tiles = peers * per
    twist_re = twist_ref[0]
    twist_im = twist_ref[1]

    def tile_of(ref):
        return lambda i: ref[i // per, :, (i % per) * LANES : (i % per + 1) * LANES]

    put_rows(tile_of(past_ref), rows_ref, chans, tiles, 0)
    put_rows(tile_of(own_ref), rows_ref, chans, tiles, tiles)
    data = by_channel(rows_ref, chans, 0, 2 * tiles)
    freq = forward(into_ref[...], cols_in_ref[...], twist_re, twist_im, data.astype(jnp.bfloat16), chans)
    spec = spec_ref[...]
    fre, fim = freq[:, :LANES], freq[:, LANES:]
    sre, sim = spec[:, :LANES], spec[:, LANES:]
    prod = jnp.concatenate([fre * sre - fim * sim, fre * sim + fim * sre], axis=1)
    last = dot(prod.astype(jnp.bfloat16), cols_out_ref[...])
    spun = []
    for c in range(chans):
        re = last[c * HALF : (c + 1) * HALF, :LANES]
        im = last[c * HALF : (c + 1) * HALF, LANES:]
        spun.append(
            jnp.concatenate(
                [re * twist_re + im * twist_im, im * twist_re - re * twist_im], axis=0
            ).astype(jnp.bfloat16)
        )
    result = dot(back_ref[...], jnp.concatenate(spun, axis=1))
    for c in range(chans):
        lanes = slice(c * LANES, (c + 1) * LANES)
        rows_ref[pl.ds(c, tiles, stride=chans), :] = (
            result[:, lanes] + gain_ref[c] * data[tiles:, lanes]
        )
    for tile in range(tiles):
        out_ref[tile // per, :, (tile % per) * LANES : (tile % per + 1) * LANES] = rows_ref[
            pl.ds(tile * chans, chans), :
        ].astype(jnp.bfloat16)


def convolve(past, own, spec, gain, into, cols_in, cols_out, back, twist):
    peers, chans, width = own.shape
    vmem = pl.BlockSpec(memory_space=pltpu.VMEM)
    return pl.pallas_call(
        convolve_kernel,
        out_shape=jax.ShapeDtypeStruct(own.shape, jnp.bfloat16),
        in_specs=[vmem, vmem, vmem, pl.BlockSpec(memory_space=pltpu.SMEM)] + [vmem] * 5,
        out_specs=vmem,
        scratch_shapes=[pltpu.VMEM((2 * peers * chans * width // LANES, LANES), jnp.float32)],
        compiler_params=pltpu.CompilerParams(vmem_limit_bytes=32 << 20),
        cost_estimate=pl.CostEstimate(
            flops=800_000_000, bytes_accessed=4 << 20, transcendentals=0
        ),
        name="convolve",
    )(past, own, spec, gain, into, cols_in, cols_out, back, twist)


def output_kernel(conv_ref, query_ref, w_ref, out_ref):
    conv = jnp.transpose(conv_ref[...].astype(jnp.float32), (1, 0))
    gated = (query_ref[...] * conv).astype(jnp.bfloat16)
    out_ref[...] = dot(gated, w_ref[...]).astype(jnp.bfloat16)


def project_out(conv, query, w_out):
    rows = query.shape[0]
    return pl.pallas_call(
        output_kernel,
        out_shape=jax.ShapeDtypeStruct((rows, D), jnp.bfloat16),
        compiler_params=pltpu.CompilerParams(vmem_limit_bytes=16 << 20),
        cost_estimate=pl.CostEstimate(
            flops=2 * rows * D * D, bytes_accessed=2 << 20, transcendentals=0
        ),
        name="project_out",
    )(conv, query, w_out)


def passed_along(array, axis):
    peers = lax.axis_size(axis)
    return lax.ppermute(array, axis, [(i, i + 1) for i in range(peers - 1)])


def per_device(tokens, w_in, short_filter, long_filter, skip_gain, w_out):
    rows = tokens.shape[0]
    peers = lax.axis_size("tok")
    into, cols_in, cols_out, back, twist = dft_tables()
    rim = passed_along(tokens[rows - RIM :], ("span", "tok"))
    product, query = project(tokens, rim, w_in, short_filter)
    own = lax.all_to_all(
        product.reshape(peers, D // peers, rows), "tok", split_axis=0, concat_axis=0, tiled=True
    )
    past = passed_along(own, "span")
    spec = spectrum(long_filter, into, cols_in, twist)
    conv = convolve(past, own, spec, skip_gain, into, cols_in, cols_out, back, twist)
    conv = lax.all_to_all(conv, "tok", split_axis=0, concat_axis=0, tiled=True)
    return project_out(conv.reshape(D, rows), query, w_out)


def solution(mesh):
    return jax.shard_map(
        per_device,
        mesh=mesh,
        in_specs=(P(("span", "tok"), None), P(), P(), P("tok", None), P("tok"), P()),
        out_specs=P(("span", "tok"), None),
        check_vma=False,
    )
```

```python
import jax
import jax.numpy as jnp
import numpy as np
from jax import lax
from jax.experimental import pallas as pl
from jax.experimental.pallas import tpu as pltpu
from jax.sharding import PartitionSpec as P

D = 256
LANES = 128
HALF = 64
RIM = 16
POINTS = LANES * LANES


def dft_tables():
    ka = np.arange(HALF) + 0.5
    idx = np.arange(LANES)
    wave = lambda phase: np.exp(-2j * np.pi * phase)
    rows = wave(np.outer(ka, idx) / LANES)
    twist = wave(np.outer(ka, idx) / POINTS)
    cols = wave(np.outer(idx, idx) / LANES)
    into = np.concatenate([rows.real, rows.imag], 0)
    back = into.T[HALF:] * (2.0 / POINTS)
    cols_in = np.block([[cols.real, cols.imag], [-cols.imag, cols.real]])
    cols_out = np.block([[cols.real.T, -cols.imag.T], [cols.imag.T, cols.real.T]])
    bf = lambda a: jnp.asarray(a.astype(np.float32)).astype(jnp.bfloat16)
    twist = np.stack([twist.real, twist.imag]).astype(np.float32)
    return bf(into), bf(cols_in), bf(cols_out), bf(back), jnp.asarray(twist)


def dot(a, b):
    return jnp.dot(a, b, preferred_element_type=jnp.float32)


VMEM = pl.BlockSpec(memory_space=pltpu.VMEM)
SMEM = pl.BlockSpec(memory_space=pltpu.SMEM)
HBM = pl.BlockSpec(memory_space=pltpu.MemorySpace.HBM)
HEAD = 8


def short_filter_sum(taps, now, one, two):
    return taps[0:1] * now + taps[1:2] * one + taps[2:3] * two


def rounded(projected):
    return projected.astype(jnp.bfloat16).astype(jnp.float32)


def project_kernel(
    tokens_hbm, w_hbm, taps_hbm, product_ref, query_ref, head_ref, w_ref, taps_ref, tokens_ref, sems
):
    copies = [
        pltpu.make_async_copy(tokens_hbm, tokens_ref, sems.at[0]),
        pltpu.make_async_copy(w_hbm, w_ref, sems.at[1]),
        pltpu.make_async_copy(taps_hbm, taps_ref, sems.at[2]),
    ]
    for copy in copies:
        copy.start()
    for copy in copies:
        copy.wait()

    def mixed(part):
        cols = slice(part * D, (part + 1) * D)
        now = rounded(dot(tokens_ref[...], w_ref[:, cols]))
        head_ref[:, cols] = now[:HEAD]
        return short_filter_sum(
            taps_ref[:, cols], now, pltpu.roll(now, 1, axis=0), pltpu.roll(now, 2, axis=0)
        )

    product = mixed(1) * mixed(2)
    product_ref[...] = jnp.transpose(product, (1, 0)).astype(jnp.bfloat16)
    query_ref[...] = mixed(0)


def project(tokens, w_in, short_filter):
    rows = tokens.shape[0]
    return pl.pallas_call(
        project_kernel,
        out_shape=(
            jax.ShapeDtypeStruct((D, rows), jnp.bfloat16),
            jax.ShapeDtypeStruct((rows, D), jnp.float32),
            jax.ShapeDtypeStruct((HEAD, 3 * D), jnp.float32),
            jax.ShapeDtypeStruct(w_in.shape, w_in.dtype),
            jax.ShapeDtypeStruct(short_filter.shape, short_filter.dtype),
        ),
        in_specs=[HBM] * 3,
        out_specs=(VMEM,) * 5,
        scratch_shapes=[pltpu.VMEM(tokens.shape, tokens.dtype), pltpu.SemaphoreType.DMA((3,))],
        compiler_params=pltpu.CompilerParams(vmem_limit_bytes=24 << 20),
        cost_estimate=pl.CostEstimate(
            flops=2 * rows * D * 3 * D, bytes_accessed=2 << 20, transcendentals=0
        ),
        name="project",
    )(tokens, w_in, short_filter)


def rim_kernel(place_ref, rim_ref, w_ref, taps_ref, head_ref, raw_ref, product_ref, query_ref):
    there = place_ref[0] + place_ref[1] > 0
    before = rounded(dot(rim_ref[...], w_ref[...]))[RIM - HEAD :]
    before = jnp.where(there, before, 0.0)
    both = jnp.concatenate([before, head_ref[...]], axis=0)
    mixed = short_filter_sum(
        taps_ref[...], both, pltpu.roll(both, 1, axis=0), pltpu.roll(both, 2, axis=0)
    )[HEAD:]
    query_ref[...] = mixed[:, :D]
    fixed = mixed[:, D : 2 * D] * mixed[:, 2 * D :]
    fixed = jnp.concatenate([fixed, jnp.zeros((LANES - HEAD, D), jnp.float32)], axis=0)
    fixed = jnp.transpose(fixed, (1, 0)).astype(jnp.bfloat16)
    lane = lax.broadcasted_iota(jnp.int32, fixed.shape, 1)
    product_ref[:, LANES:] = raw_ref[:, LANES:]
    product_ref[:, :LANES] = jnp.where(lane < HEAD, fixed, raw_ref[:, :LANES])


def fix_rim(place, rim, w_in, short_filter, head, product):
    return pl.pallas_call(
        rim_kernel,
        out_shape=(
            jax.ShapeDtypeStruct(product.shape, product.dtype),
            jax.ShapeDtypeStruct((HEAD, D), jnp.float32),
        ),
        in_specs=[SMEM] + [VMEM] * 5,
        out_specs=(VMEM, VMEM),
        compiler_params=pltpu.CompilerParams(vmem_limit_bytes=16 << 20),
        cost_estimate=pl.CostEstimate(flops=20_000_000, bytes_accessed=1 << 20, transcendentals=0),
        name="fix_rim",
    )(place, rim, w_in, short_filter, head, product)


def put_rows(load, scratch, chans, tiles, at):
    for tile in range(tiles):
        scratch[pl.ds((at + tile) * chans, chans), :] = load(tile).astype(jnp.float32)


def by_channel(scratch, chans, at, tiles):
    return jnp.concatenate(
        [scratch[pl.ds(at * chans + c, tiles, stride=chans), :] for c in range(chans)], axis=1
    )


def forward(into, cols_in, twist_re, twist_im, data, chans):
    first = dot(into, data)
    spun = []
    for c in range(chans):
        re = first[:HALF, c * LANES : (c + 1) * LANES]
        im = first[HALF:, c * LANES : (c + 1) * LANES]
        spun.append(
            jnp.concatenate(
                [re * twist_re - im * twist_im, re * twist_im + im * twist_re], axis=1
            ).astype(jnp.bfloat16)
        )
    return dot(jnp.concatenate(spun, axis=0), cols_in)


def spectrum_kernel(filter_ref, into_ref, cols_in_ref, twist_ref, out_ref, rows_ref):
    chans, taps = filter_ref.shape
    tiles = taps // LANES
    put_rows(lambda i: filter_ref[:, i * LANES : (i + 1) * LANES], rows_ref, chans, tiles, 0)
    data = by_channel(rows_ref, chans, 0, tiles).astype(jnp.bfloat16)
    out_ref[...] = forward(
        into_ref[:, :tiles], cols_in_ref[...], twist_ref[0], twist_ref[1], data, chans
    )


def spectrum(long_filter, into, cols_in, twist):
    chans, taps = long_filter.shape
    return pl.pallas_call(
        spectrum_kernel,
        out_shape=jax.ShapeDtypeStruct((chans * HALF, 2 * LANES), jnp.float32),
        scratch_shapes=[pltpu.VMEM((taps // LANES * chans, LANES), jnp.float32)],
        compiler_params=pltpu.CompilerParams(vmem_limit_bytes=24 << 20),
        cost_estimate=pl.CostEstimate(
            flops=400_000_000, bytes_accessed=3 << 20, transcendentals=0
        ),
        name="spectrum",
    )(long_filter, into, cols_in, twist)


def convolve_kernel(
    place_ref, past_ref, own_ref, spec_ref, gain_ref, into_ref, cols_in_ref, cols_out_ref, back_ref,
    twist_ref, out_ref, rows_ref,
):
    peers, chans, width = own_ref.shape
    per = width // LANES
    tiles = peers * per
    twist_re = twist_ref[0]
    twist_im = twist_ref[1]

    def tile_of(ref):
        return lambda i: ref[i // per, :, (i % per) * LANES : (i % per + 1) * LANES]

    put_rows(tile_of(past_ref), rows_ref, chans, tiles, 0)

    @pl.when(place_ref[0] == 0)
    def _():
        rows_ref[: tiles * chans] = jnp.zeros((tiles * chans, LANES), jnp.float32)

    put_rows(tile_of(own_ref), rows_ref, chans, tiles, tiles)
    data = by_channel(rows_ref, chans, 0, 2 * tiles)
    freq = forward(into_ref[...], cols_in_ref[...], twist_re, twist_im, data.astype(jnp.bfloat16), chans)
    spec = spec_ref[...]
    fre, fim = freq[:, :LANES], freq[:, LANES:]
    sre, sim = spec[:, :LANES], spec[:, LANES:]
    prod = jnp.concatenate([fre * sre - fim * sim, fre * sim + fim * sre], axis=1)
    last = dot(prod.astype(jnp.bfloat16), cols_out_ref[...])
    spun = []
    for c in range(chans):
        re = last[c * HALF : (c + 1) * HALF, :LANES]
        im = last[c * HALF : (c + 1) * HALF, LANES:]
        spun.append(
            jnp.concatenate(
                [re * twist_re + im * twist_im, im * twist_re - re * twist_im], axis=0
            ).astype(jnp.bfloat16)
        )
    result = dot(back_ref[...], jnp.concatenate(spun, axis=1))
    for c in range(chans):
        lanes = slice(c * LANES, (c + 1) * LANES)
        rows_ref[pl.ds(c, tiles, stride=chans), :] = (
            result[:, lanes] + gain_ref[c] * data[tiles:, lanes]
        )
    for tile in range(tiles):
        out_ref[tile // per, :, (tile % per) * LANES : (tile % per + 1) * LANES] = rows_ref[
            pl.ds(tile * chans, chans), :
        ].astype(jnp.bfloat16)


def convolve(place, past, own, spec, gain, into, cols_in, cols_out, back, twist):
    peers, chans, width = own.shape
    return pl.pallas_call(
        convolve_kernel,
        out_shape=jax.ShapeDtypeStruct(own.shape, jnp.bfloat16),
        in_specs=[SMEM] + [VMEM] * 3 + [SMEM] + [VMEM] * 5,
        out_specs=VMEM,
        scratch_shapes=[pltpu.VMEM((2 * peers * chans * width // LANES, LANES), jnp.float32)],
        compiler_params=pltpu.CompilerParams(vmem_limit_bytes=32 << 20),
        cost_estimate=pl.CostEstimate(
            flops=800_000_000, bytes_accessed=4 << 20, transcendentals=0
        ),
        name="convolve",
    )(place, past, own, spec, gain, into, cols_in, cols_out, back, twist)


def output_kernel(conv_ref, query_ref, head_ref, w_ref, out_ref):
    conv = jnp.transpose(conv_ref[...].astype(jnp.float32), (1, 0))
    query = jnp.concatenate([head_ref[...], query_ref[HEAD:]], axis=0)
    gated = (query * conv).astype(jnp.bfloat16)
    out_ref[...] = dot(gated, w_ref[...]).astype(jnp.bfloat16)


def project_out(conv, query, head, w_out):
    rows = query.shape[0]
    return pl.pallas_call(
        output_kernel,
        out_shape=jax.ShapeDtypeStruct((rows, D), jnp.bfloat16),
        compiler_params=pltpu.CompilerParams(vmem_limit_bytes=16 << 20),
        cost_estimate=pl.CostEstimate(
            flops=2 * rows * D * D, bytes_accessed=2 << 20, transcendentals=0
        ),
        name="project_out",
    )(conv, query, head, w_out)


def rotated(array, axes):
    count = lax.axis_size(axes)
    return lax.ppermute(array, axes, [(i, (i + 1) % count) for i in range(count)])


def per_device(tokens, w_in, short_filter, long_filter, skip_gain, w_out):
    rows = tokens.shape[0]
    peers = lax.axis_size("tok")
    into, cols_in, cols_out, back, twist = dft_tables()
    place = jnp.stack([lax.axis_index("span"), lax.axis_index("tok")]).astype(jnp.int32)
    rim = rotated(tokens[rows - RIM :], ("span", "tok"))
    product, query, head, w_copy, taps = project(tokens, w_in, short_filter)
    product, query_head = fix_rim(place, rim, w_copy, taps, head, product)
    own = lax.all_to_all(
        product.reshape(peers, D // peers, rows), "tok", split_axis=0, concat_axis=0, tiled=True
    )
    past = rotated(own, "span")
    spec = spectrum(long_filter, into, cols_in, twist)
    conv = convolve(place, past, own, spec, skip_gain, into, cols_in, cols_out, back, twist)
    conv = lax.all_to_all(conv, "tok", split_axis=0, concat_axis=0, tiled=True)
    return project_out(conv.reshape(D, rows), query, query_head, w_out)


def solution(mesh):
    return jax.shard_map(
        per_device,
        mesh=mesh,
        in_specs=(P(("span", "tok"), None), P(), P(), P("tok", None), P("tok"), P()),
        out_specs=P(("span", "tok"), None),
        check_vma=False,
    )
```

```python
import jax
import jax.numpy as jnp
import numpy as np
from jax import lax
from jax.experimental import pallas as pl
from jax.experimental.pallas import tpu as pltpu
from jax.sharding import PartitionSpec as P

D = 256
LANES = 128
HALF = 64
RIM = 16
POINTS = LANES * LANES


def dft_tables():
    ka = np.arange(HALF) + 0.5
    idx = np.arange(LANES)
    wave = lambda phase: np.exp(-2j * np.pi * phase)
    rows = wave(np.outer(ka, idx) / LANES)
    twist = wave(np.outer(ka, idx) / POINTS)
    cols = wave(np.outer(idx, idx) / LANES)
    into = np.concatenate([rows.real, rows.imag], 0)
    back = into.T[HALF:] * (2.0 / POINTS)
    cols_in = np.block([[cols.real, cols.imag], [-cols.imag, cols.real]])
    cols_out = np.block([[cols.real.T, -cols.imag.T], [cols.imag.T, cols.real.T]])
    bf = lambda a: a.astype(np.float32).astype(jnp.bfloat16)
    pair = lambda a: np.concatenate([bf(a), bf(a - bf(a).astype(np.float64))], 1)
    twist = np.stack([twist.real, twist.imag]).astype(np.float32)
    tables = pair(into[:, :HALF]), pair(into[:, HALF:]), bf(cols_in), bf(cols_out), pair(back), twist
    return [jnp.asarray(table) for table in tables]


def dot(a, b):
    return jnp.dot(a, b, preferred_element_type=jnp.float32)


VMEM = pl.BlockSpec(memory_space=pltpu.VMEM)
HBM = pl.BlockSpec(memory_space=pltpu.MemorySpace.HBM)
HEAD = 8
PIECES = 4


def short_filter_sum(taps, now, one, two):
    return taps[0:1] * now + taps[1:2] * one + taps[2:3] * two


def rounded(projected):
    return projected.astype(jnp.bfloat16).astype(jnp.float32)


def project_kernel(
    tokens_hbm, w_hbm, taps_hbm, product_ref, head_ref, w_ref, taps_ref, tokens_ref, sems
):
    copies = [
        pltpu.make_async_copy(w_hbm.at[:, pl.ds(D, 2 * D)], w_ref, sems.at[0]),
        pltpu.make_async_copy(tokens_hbm, tokens_ref, sems.at[1]),
        pltpu.make_async_copy(taps_hbm, taps_ref, sems.at[2]),
    ]
    for copy in copies:
        copy.start()
    for copy in copies:
        copy.wait()

    def mixed(part):
        cols = slice(part * D, (part + 1) * D)
        now = rounded(dot(tokens_ref[...], w_ref[:, cols]))
        head_ref[:, cols] = now[:HEAD]
        taps = taps_ref[:, (part + 1) * D : (part + 2) * D]
        return short_filter_sum(taps, now, pltpu.roll(now, 1, axis=0), pltpu.roll(now, 2, axis=0))

    product = mixed(0) * mixed(1)
    product_ref[...] = jnp.transpose(product, (1, 0)).astype(jnp.bfloat16)


def project(tokens, w_in, short_filter):
    rows = tokens.shape[0]
    inputs = [
        pltpu.with_memory_space_constraint(a, pltpu.MemorySpace.HBM)
        for a in (tokens, w_in, short_filter)
    ]
    return pl.pallas_call(
        project_kernel,
        out_shape=(
            jax.ShapeDtypeStruct((D, rows), jnp.bfloat16),
            jax.ShapeDtypeStruct((HEAD, 2 * D), jnp.float32),
            jax.ShapeDtypeStruct((D, 2 * D), w_in.dtype),
            jax.ShapeDtypeStruct(short_filter.shape, short_filter.dtype),
        ),
        in_specs=[HBM] * 3,
        out_specs=(VMEM,) * 4,
        scratch_shapes=[pltpu.VMEM(tokens.shape, tokens.dtype), pltpu.SemaphoreType.DMA((3,))],
        compiler_params=pltpu.CompilerParams(vmem_limit_bytes=24 << 20),
        cost_estimate=pl.CostEstimate(
            flops=2 * rows * D * 2 * D, bytes_accessed=2 << 20, transcendentals=0
        ),
        name="project",
    )(*inputs)


def rim_kernel(there_ref, rim_ref, w_ref, taps_ref, head_ref, raw_ref, product_ref):
    before = rounded(dot(rim_ref[...], w_ref[...]))[RIM - HEAD :]
    there = jnp.concatenate([there_ref[0:1], there_ref[0:1]], axis=1)
    before = jnp.where(there > 0.0, before, 0.0)
    both = jnp.concatenate([before, head_ref[...]], axis=0)
    mixed = short_filter_sum(
        taps_ref[:, D:], both, pltpu.roll(both, 1, axis=0), pltpu.roll(both, 2, axis=0)
    )[HEAD:]
    fixed = mixed[:, :D] * mixed[:, D:]
    fixed = jnp.concatenate([fixed, jnp.zeros((LANES - HEAD, D), jnp.float32)], axis=0)
    fixed = jnp.transpose(fixed, (1, 0)).astype(jnp.bfloat16)
    lane = lax.broadcasted_iota(jnp.int32, fixed.shape, 1)
    product_ref[:, LANES:] = raw_ref[:, LANES:]
    product_ref[:, :LANES] = jnp.where(lane < HEAD, fixed, raw_ref[:, :LANES])


def fix_rim(there, rim, w_part, short_filter, head, product):
    return pl.pallas_call(
        rim_kernel,
        out_shape=jax.ShapeDtypeStruct(product.shape, product.dtype),
        in_specs=[VMEM] * 6,
        out_specs=VMEM,
        compiler_params=pltpu.CompilerParams(vmem_limit_bytes=16 << 20),
        cost_estimate=pl.CostEstimate(flops=20_000_000, bytes_accessed=1 << 20, transcendentals=0),
        name="fix_rim",
    )(there, rim, w_part, short_filter, head, product)


def query_kernel(there_ref, tokens_ref, rim_ref, w_ref, taps_ref, query_ref):
    weights = w_ref[:, :D]
    taps = taps_ref[:, :D]
    now = rounded(dot(tokens_ref[...], weights))
    query_ref[...] = short_filter_sum(
        taps, now, pltpu.roll(now, 1, axis=0), pltpu.roll(now, 2, axis=0)
    )
    before = rounded(dot(rim_ref[...], weights))[RIM - HEAD :]
    both = jnp.concatenate([jnp.where(there_ref[0:1] > 0.0, before, 0.0), now[:HEAD]], axis=0)
    query_ref[:HEAD] = short_filter_sum(
        taps, both, pltpu.roll(both, 1, axis=0), pltpu.roll(both, 2, axis=0)
    )[HEAD:]


def make_query(there, tokens, rim, w_in, short_filter):
    rows = tokens.shape[0]
    return pl.pallas_call(
        query_kernel,
        out_shape=jax.ShapeDtypeStruct((rows, D), jnp.float32),
        in_specs=[VMEM] * 5,
        out_specs=VMEM,
        compiler_params=pltpu.CompilerParams(vmem_limit_bytes=16 << 20),
        cost_estimate=pl.CostEstimate(
            flops=2 * rows * D * D, bytes_accessed=1 << 20, transcendentals=0
        ),
        name="make_query",
    )(there, tokens, rim, w_in, short_filter)


def put_rows(load, scratch, chans, tiles, at):
    for tile in range(tiles):
        scratch[pl.ds((at + tile) * chans, chans), :] = load(tile).astype(jnp.float32)


def by_channel(scratch, chans, at, tiles):
    return jnp.concatenate(
        [scratch[pl.ds(at * chans + c, tiles, stride=chans), :] for c in range(chans)], axis=1
    )


def forward(into, cols_in, twist_re, twist_im, data, chans):
    first = dot(into, jnp.concatenate([data, data], axis=0))
    spun = []
    for c in range(chans):
        re = first[:HALF, c * LANES : (c + 1) * LANES]
        im = first[HALF:, c * LANES : (c + 1) * LANES]
        spun.append(
            jnp.concatenate(
                [re * twist_re - im * twist_im, re * twist_im + im * twist_re], axis=1
            ).astype(jnp.bfloat16)
        )
    return dot(jnp.concatenate(spun, axis=0), cols_in)


def rows_of(ref):
    per = ref.shape[2] // LANES
    return lambda i: ref[i // per, :, (i % per) * LANES : (i % per + 1) * LANES]


def early_kernel(
    filter_ref, own_ref, gain_ref, into_lo_ref, into_hi_ref, cols_in_ref, twist_ref, spec_ref,
    freq_ref, skip_ref, rows_ref,
):
    chans, taps = filter_ref.shape
    tiles = taps // LANES
    put_rows(lambda i: filter_ref[:, i * LANES : (i + 1) * LANES], rows_ref, chans, tiles, 0)
    gain = jnp.broadcast_to(gain_ref[...], (chans, LANES))
    per = own_ref.shape[2] // LANES
    for tile in range(tiles):
        lanes = slice(tile % per * LANES, (tile % per + 1) * LANES)
        own = own_ref[tile // per, :, lanes].astype(jnp.float32)
        rows_ref[pl.ds((tiles + tile) * chans, chans), :] = own
        skip_ref[tile // per, :, lanes] = gain * own
    twist = twist_ref[0], twist_ref[1]
    data = by_channel(rows_ref, chans, 0, tiles).astype(jnp.bfloat16)
    spec_ref[...] = forward(into_lo_ref[...], cols_in_ref[...], *twist, data, chans)
    data = by_channel(rows_ref, chans, tiles, tiles)
    freq_ref[...] = forward(
        into_hi_ref[...], cols_in_ref[...], *twist, data.astype(jnp.bfloat16), chans
    )


def early(long_filter, own, gain, into_lo, into_hi, cols_in, twist):
    chans, taps = long_filter.shape
    tiles = taps // LANES
    points = jax.ShapeDtypeStruct((chans * HALF, 2 * LANES), jnp.float32)
    return pl.pallas_call(
        early_kernel,
        out_shape=(points, points, jax.ShapeDtypeStruct(own.shape, jnp.float32)),
        in_specs=[VMEM] * 7,
        out_specs=(VMEM,) * 3,
        scratch_shapes=[pltpu.VMEM((2 * tiles * chans, LANES), jnp.float32)],
        compiler_params=pltpu.CompilerParams(vmem_limit_bytes=24 << 20),
        cost_estimate=pl.CostEstimate(
            flops=800_000_000, bytes_accessed=3 << 20, transcendentals=0
        ),
        name="early",
    )(long_filter, own, gain, into_lo, into_hi, cols_in, twist)


def convolve_kernel(
    there_ref, past_ref, spec_ref, freq_ref, skip_ref, into_lo_ref, cols_in_ref, cols_out_ref,
    back_ref, twist_ref, out_ref, rows_ref,
):
    peers, chans, width = out_ref.shape
    per = width // LANES
    tiles = peers * per
    twist_re = twist_ref[0]
    twist_im = twist_ref[1]
    there = jnp.broadcast_to(there_ref[1:2, :LANES], (chans, LANES)) > 0.0
    load = rows_of(past_ref)
    put_rows(lambda i: jnp.where(there, load(i).astype(jnp.float32), 0.0), rows_ref, chans, tiles, 0)
    past = by_channel(rows_ref, chans, 0, tiles).astype(jnp.bfloat16)
    freq = forward(into_lo_ref[...], cols_in_ref[...], twist_re, twist_im, past, chans) + freq_ref[...]
    spec = spec_ref[...]
    fre, fim = freq[:, :LANES], freq[:, LANES:]
    sre, sim = spec[:, :LANES], spec[:, LANES:]
    prod = jnp.concatenate([fre * sre - fim * sim, fre * sim + fim * sre], axis=1)
    last = dot(prod.astype(jnp.bfloat16), cols_out_ref[...])
    spun = []
    for c in range(chans):
        re = last[c * HALF : (c + 1) * HALF, :LANES]
        im = last[c * HALF : (c + 1) * HALF, LANES:]
        spun.append(
            jnp.concatenate(
                [re * twist_re + im * twist_im, im * twist_re - re * twist_im], axis=0
            ).astype(jnp.bfloat16)
        )
    spun = jnp.concatenate(spun, axis=1)
    result = dot(back_ref[...], jnp.concatenate([spun, spun], axis=0))
    for c in range(chans):
        lanes = slice(c * LANES, (c + 1) * LANES)
        rows_ref[pl.ds(c, tiles, stride=chans), :] = result[:, lanes]
    for tile in range(tiles):
        lanes = slice(tile % per * LANES, (tile % per + 1) * LANES)
        out = rows_ref[pl.ds(tile * chans, chans), :] + skip_ref[tile // per, :, lanes]
        out_ref[tile // per, :, lanes] = out.astype(jnp.bfloat16)


def convolve(there, past, spec, freq, skip, into_lo, cols_in, cols_out, back, twist):
    peers, chans, width = past.shape
    return pl.pallas_call(
        convolve_kernel,
        out_shape=jax.ShapeDtypeStruct(past.shape, jnp.bfloat16),
        in_specs=[VMEM] * 10,
        out_specs=VMEM,
        scratch_shapes=[pltpu.VMEM((peers * chans * width // LANES, LANES), jnp.float32)],
        compiler_params=pltpu.CompilerParams(vmem_limit_bytes=32 << 20),
        cost_estimate=pl.CostEstimate(
            flops=800_000_000, bytes_accessed=4 << 20, transcendentals=0
        ),
        name="convolve",
    )(there, past, spec, freq, skip, into_lo, cols_in, cols_out, back, twist)


def output_kernel(conv_ref, query_ref, w_ref, out_hbm, out_ref, sems):
    rows = query_ref.shape[0] // PIECES
    copies = []
    for piece in range(PIECES):
        at = slice(piece * rows, (piece + 1) * rows)
        conv = jnp.transpose(conv_ref[:, at].astype(jnp.float32), (1, 0))
        gated = (query_ref[at] * conv).astype(jnp.bfloat16)
        out_ref[at] = dot(gated, w_ref[...]).astype(jnp.bfloat16)
        copies.append(pltpu.make_async_copy(out_ref.at[at], out_hbm.at[at], sems.at[piece]))
        copies[-1].start()
    for copy in copies:
        copy.wait()


def project_out(conv, query, w_out):
    rows = query.shape[0]
    return pl.pallas_call(
        output_kernel,
        out_shape=jax.ShapeDtypeStruct((rows, D), jnp.bfloat16),
        in_specs=[VMEM] * 3,
        out_specs=HBM,
        scratch_shapes=[
            pltpu.VMEM((rows, D), jnp.bfloat16), pltpu.SemaphoreType.DMA((PIECES,))
        ],
        compiler_params=pltpu.CompilerParams(vmem_limit_bytes=16 << 20),
        cost_estimate=pl.CostEstimate(
            flops=2 * rows * D * D, bytes_accessed=2 << 20, transcendentals=0
        ),
        name="project_out",
    )(conv, query, w_out)


def rotated(array, axes):
    count = lax.axis_size(axes)
    return lax.ppermute(array, axes, [(i, (i + 1) % count) for i in range(count)])


def per_device(tokens, w_in, short_filter, long_filter, skip_gain, w_out):
    rows = tokens.shape[0]
    peers = lax.axis_size("tok")
    into_lo, into_hi, cols_in, cols_out, back, twist = dft_tables()
    span = lax.axis_index("span")
    there = jnp.stack([span + lax.axis_index("tok") > 0, span > 0]).astype(jnp.float32)
    there = jnp.broadcast_to(there[:, None], (2, D))
    rim = rotated(tokens[rows - RIM :], ("span", "tok"))
    product, head, w_part, taps = project(tokens, w_in, short_filter)
    product = fix_rim(there, rim, w_part, taps, head, product)
    own = lax.all_to_all(
        product.reshape(peers, D // peers, rows), "tok", split_axis=0, concat_axis=0, tiled=True
    )
    past = rotated(own, "span")
    spec, freq, skip = early(long_filter, own, skip_gain.reshape(-1, 1), into_lo, into_hi, cols_in, twist)
    query = make_query(there, tokens, rim, w_in, short_filter)
    freq, query = lax.optimization_barrier((freq, query))
    conv = convolve(there, past, spec, freq, skip, into_lo, cols_in, cols_out, back, twist)
    conv = lax.all_to_all(conv, "tok", split_axis=0, concat_axis=0, tiled=True)
    return project_out(conv.reshape(D, rows), query, w_out)


def solution(mesh):
    return jax.shard_map(
        per_device,
        mesh=mesh,
        in_specs=(P(("span", "tok"), None), P(), P(), P("tok", None), P("tok"), P()),
        out_specs=P(("span", "tok"), None),
        check_vma=False,
    )
```

```python
import jax
import jax.numpy as jnp
import numpy as np
from jax import lax
from jax.experimental import pallas as pl
from jax.experimental.pallas import tpu as pltpu
from jax.sharding import PartitionSpec as P

D = 256
LANES = 128
HALF = 64
RIM = 16
POINTS = LANES * LANES


def dft_tables():
    ka = np.arange(HALF) + 0.5
    idx = np.arange(LANES)
    wave = lambda phase: np.exp(-2j * np.pi * phase)
    rows = wave(np.outer(ka, idx) / LANES)
    twist = wave(np.outer(ka, idx) / POINTS)
    cols = wave(np.outer(idx, idx) / LANES)
    into = np.concatenate([rows.real, rows.imag], 0)
    back = into.T[HALF:] * (2.0 / POINTS)
    cols_in = np.block([[cols.real, cols.imag], [-cols.imag, cols.real]])
    cols_out = np.block([[cols.real.T, -cols.imag.T], [cols.imag.T, cols.real.T]])
    bf = lambda a: a.astype(np.float32).astype(jnp.bfloat16)
    pair = lambda a: np.concatenate([bf(a), bf(a - bf(a).astype(np.float64))], 1)
    twist = np.stack([twist.real, twist.imag]).astype(np.float32)
    high = bf(cols_in)
    wide = np.concatenate([high, bf(cols_in - high.astype(np.float64)), high], 0)
    tables = pair(into[:, :HALF]), pair(into[:, HALF:]), high, wide, bf(cols_out), pair(back), twist
    return [jnp.asarray(table) for table in tables]


def dot(a, b):
    return jnp.dot(a, b, preferred_element_type=jnp.float32)


VMEM = pl.BlockSpec(memory_space=pltpu.VMEM)
HBM = pl.BlockSpec(memory_space=pltpu.MemorySpace.HBM)
HEAD = 8
PIECES = 2


def short_filter_sum(taps, now, one, two):
    return taps[0:1] * now + taps[1:2] * one + taps[2:3] * two


def rounded(projected):
    return projected.astype(jnp.bfloat16).astype(jnp.float32)


def project_kernel(
    tokens_hbm, w_hbm, taps_hbm, product_ref, head_ref, w_ref, taps_ref, tokens_ref, sems
):
    copies = [
        pltpu.make_async_copy(w_hbm.at[:, pl.ds(D, 2 * D)], w_ref, sems.at[0]),
        pltpu.make_async_copy(tokens_hbm, tokens_ref, sems.at[1]),
        pltpu.make_async_copy(taps_hbm, taps_ref, sems.at[2]),
    ]
    for copy in copies:
        copy.start()
    for copy in copies:
        copy.wait()

    now = rounded(dot(tokens_ref[...], w_ref[...]))
    head_ref[...] = now[:HEAD]
    mixed = short_filter_sum(
        taps_ref[:, D:], now, pltpu.roll(now, 1, axis=0), pltpu.roll(now, 2, axis=0)
    )
    product = mixed[:, :D] * mixed[:, D:]
    product_ref[...] = jnp.transpose(product, (1, 0)).astype(jnp.bfloat16)


def project(tokens, w_in, short_filter):
    rows = tokens.shape[0]
    inputs = [
        pltpu.with_memory_space_constraint(a, pltpu.MemorySpace.HBM)
        for a in (tokens, w_in, short_filter)
    ]
    return pl.pallas_call(
        project_kernel,
        out_shape=(
            jax.ShapeDtypeStruct((D, rows), jnp.bfloat16),
            jax.ShapeDtypeStruct((HEAD, 2 * D), jnp.float32),
            jax.ShapeDtypeStruct((D, 2 * D), w_in.dtype),
            jax.ShapeDtypeStruct(short_filter.shape, short_filter.dtype),
        ),
        in_specs=[HBM] * 3,
        out_specs=(VMEM,) * 4,
        scratch_shapes=[pltpu.VMEM(tokens.shape, tokens.dtype), pltpu.SemaphoreType.DMA((3,))],
        compiler_params=pltpu.CompilerParams(vmem_limit_bytes=24 << 20),
        cost_estimate=pl.CostEstimate(
            flops=2 * rows * D * 2 * D, bytes_accessed=2 << 20, transcendentals=0
        ),
        name="project",
    )(*inputs)


def rim_kernel(there_ref, rim_ref, w_ref, taps_ref, head_ref, raw_ref, product_ref):
    before = rounded(dot(rim_ref[...], w_ref[...]))[RIM - HEAD :]
    there = jnp.concatenate([there_ref[0:1], there_ref[0:1]], axis=1)
    before = jnp.where(there > 0.0, before, 0.0)
    both = jnp.concatenate([before, head_ref[...]], axis=0)
    mixed = short_filter_sum(
        taps_ref[:, D:], both, pltpu.roll(both, 1, axis=0), pltpu.roll(both, 2, axis=0)
    )[HEAD:]
    fixed = mixed[:, :D] * mixed[:, D:]
    fixed = jnp.concatenate([fixed, jnp.zeros((LANES - HEAD, D), jnp.float32)], axis=0)
    fixed = jnp.transpose(fixed, (1, 0)).astype(jnp.bfloat16)
    lane = lax.broadcasted_iota(jnp.int32, fixed.shape, 1)
    product_ref[:, LANES:] = raw_ref[:, LANES:]
    product_ref[:, :LANES] = jnp.where(lane < HEAD, fixed, raw_ref[:, :LANES])


def fix_rim(there, rim, w_part, short_filter, head, product):
    return pl.pallas_call(
        rim_kernel,
        out_shape=jax.ShapeDtypeStruct(product.shape, product.dtype),
        in_specs=[VMEM] * 6,
        out_specs=VMEM,
        compiler_params=pltpu.CompilerParams(vmem_limit_bytes=16 << 20),
        cost_estimate=pl.CostEstimate(flops=20_000_000, bytes_accessed=1 << 20, transcendentals=0),
        name="fix_rim",
    )(there, rim, w_part, short_filter, head, product)


def query_kernel(there_ref, tokens_ref, rim_ref, w_ref, taps_ref, query_ref):
    weights = w_ref[:, :D]
    taps = taps_ref[:, :D]
    now = rounded(dot(tokens_ref[...], weights))
    query_ref[...] = short_filter_sum(
        taps, now, pltpu.roll(now, 1, axis=0), pltpu.roll(now, 2, axis=0)
    )
    before = rounded(dot(rim_ref[...], weights))[RIM - HEAD :]
    both = jnp.concatenate([jnp.where(there_ref[0:1] > 0.0, before, 0.0), now[:HEAD]], axis=0)
    query_ref[:HEAD] = short_filter_sum(
        taps, both, pltpu.roll(both, 1, axis=0), pltpu.roll(both, 2, axis=0)
    )[HEAD:]


def make_query(there, tokens, rim, w_in, short_filter):
    rows = tokens.shape[0]
    return pl.pallas_call(
        query_kernel,
        out_shape=jax.ShapeDtypeStruct((rows, D), jnp.float32),
        in_specs=[VMEM] * 5,
        out_specs=VMEM,
        compiler_params=pltpu.CompilerParams(vmem_limit_bytes=16 << 20),
        cost_estimate=pl.CostEstimate(
            flops=2 * rows * D * D, bytes_accessed=1 << 20, transcendentals=0
        ),
        name="make_query",
    )(there, tokens, rim, w_in, short_filter)


def put_rows(load, scratch, chans, tiles, at):
    for tile in range(tiles):
        scratch[pl.ds((at + tile) * chans, chans), :] = load(tile).astype(jnp.float32)


def by_channel(scratch, chans, at, tiles):
    return jnp.concatenate(
        [scratch[pl.ds(at * chans + c, tiles, stride=chans), :] for c in range(chans)], axis=1
    )


def forward(into, cols_in, twist_re, twist_im, data, chans):
    parts = cols_in.shape[0] // (2 * LANES)
    first = dot(into, jnp.concatenate([data, data], axis=0))
    spun = []
    for c in range(chans):
        re = first[:HALF, c * LANES : (c + 1) * LANES]
        im = first[HALF:, c * LANES : (c + 1) * LANES]
        turned = jnp.concatenate(
            [re * twist_re - im * twist_im, re * twist_im + im * twist_re], axis=1
        )
        high = turned.astype(jnp.bfloat16)
        row = [high] * min(parts, 2)
        if parts == 3:
            row.append((turned - high.astype(jnp.float32)).astype(jnp.bfloat16))
        spun.append(jnp.concatenate(row, axis=1) if parts > 1 else high)
    return dot(jnp.concatenate(spun, axis=0), cols_in)


def rows_of(ref):
    per = ref.shape[2] // LANES
    return lambda i: ref[i // per, :, (i % per) * LANES : (i % per + 1) * LANES]


def early_kernel(
    filter_ref, own_ref, gain_ref, into_lo_ref, into_hi_ref, cols_in_ref, twist_ref, spec_ref,
    freq_ref, skip_ref, rows_ref,
):
    chans, taps = filter_ref.shape
    tiles = taps // LANES
    put_rows(lambda i: filter_ref[:, i * LANES : (i + 1) * LANES], rows_ref, chans, tiles, 0)
    gain = jnp.broadcast_to(gain_ref[...], (chans, LANES))
    per = own_ref.shape[2] // LANES
    for tile in range(tiles):
        lanes = slice(tile % per * LANES, (tile % per + 1) * LANES)
        own = own_ref[tile // per, :, lanes].astype(jnp.float32)
        rows_ref[pl.ds((tiles + tile) * chans, chans), :] = own
        skip_ref[tile // per, :, lanes] = gain * own
    twist = twist_ref[0], twist_ref[1]
    data = by_channel(rows_ref, chans, 0, tiles).astype(jnp.bfloat16)
    spec_ref[...] = forward(into_lo_ref[...], cols_in_ref[...], *twist, data, chans)
    data = by_channel(rows_ref, chans, tiles, tiles)
    freq_ref[...] = forward(
        into_hi_ref[...], cols_in_ref[: 4 * LANES], *twist, data.astype(jnp.bfloat16), chans
    )


def early(long_filter, own, gain, into_lo, into_hi, cols_in, twist):
    chans, taps = long_filter.shape
    tiles = taps // LANES
    points = jax.ShapeDtypeStruct((chans * HALF, 2 * LANES), jnp.float32)
    return pl.pallas_call(
        early_kernel,
        out_shape=(points, points, jax.ShapeDtypeStruct(own.shape, jnp.float32)),
        in_specs=[VMEM] * 7,
        out_specs=(VMEM,) * 3,
        scratch_shapes=[pltpu.VMEM((2 * tiles * chans, LANES), jnp.float32)],
        compiler_params=pltpu.CompilerParams(vmem_limit_bytes=24 << 20),
        cost_estimate=pl.CostEstimate(
            flops=800_000_000, bytes_accessed=3 << 20, transcendentals=0
        ),
        name="early",
    )(long_filter, own, gain, into_lo, into_hi, cols_in, twist)


def convolve_kernel(
    there_ref, past_ref, spec_ref, freq_ref, skip_ref, into_lo_ref, cols_in_ref, cols_out_ref,
    back_ref, twist_ref, out_ref, rows_ref,
):
    peers, chans, width = out_ref.shape
    per = width // LANES
    tiles = peers * per
    twist_re = twist_ref[0]
    twist_im = twist_ref[1]
    there = jnp.broadcast_to(there_ref[1:2, :LANES], (chans, LANES)) > 0.0
    load = rows_of(past_ref)
    put_rows(lambda i: jnp.where(there, load(i).astype(jnp.float32), 0.0), rows_ref, chans, tiles, 0)
    past = by_channel(rows_ref, chans, 0, tiles).astype(jnp.bfloat16)
    freq = forward(into_lo_ref[...], cols_in_ref[...], twist_re, twist_im, past, chans) + freq_ref[...]
    spec = spec_ref[...]
    fre, fim = freq[:, :LANES], freq[:, LANES:]
    sre, sim = spec[:, :LANES], spec[:, LANES:]
    prod = jnp.concatenate([fre * sre - fim * sim, fre * sim + fim * sre], axis=1)
    last = dot(prod.astype(jnp.bfloat16), cols_out_ref[...])
    spun = []
    for c in range(chans):
        re = last[c * HALF : (c + 1) * HALF, :LANES]
        im = last[c * HALF : (c + 1) * HALF, LANES:]
        spun.append(
            jnp.concatenate(
                [re * twist_re + im * twist_im, im * twist_re - re * twist_im], axis=0
            ).astype(jnp.bfloat16)
        )
    spun = jnp.concatenate(spun, axis=1)
    result = dot(back_ref[...], jnp.concatenate([spun, spun], axis=0))
    for c in range(chans):
        lanes = slice(c * LANES, (c + 1) * LANES)
        rows_ref[pl.ds(c, tiles, stride=chans), :] = result[:, lanes]
    for tile in range(tiles):
        lanes = slice(tile % per * LANES, (tile % per + 1) * LANES)
        out = rows_ref[pl.ds(tile * chans, chans), :] + skip_ref[tile // per, :, lanes]
        out_ref[tile // per, :, lanes] = out.astype(jnp.bfloat16)


def convolve(there, past, spec, freq, skip, into_lo, cols_in, cols_out, back, twist):
    peers, chans, width = past.shape
    return pl.pallas_call(
        convolve_kernel,
        out_shape=jax.ShapeDtypeStruct(past.shape, jnp.bfloat16),
        in_specs=[VMEM] * 10,
        out_specs=VMEM,
        scratch_shapes=[pltpu.VMEM((peers * chans * width // LANES, LANES), jnp.float32)],
        compiler_params=pltpu.CompilerParams(vmem_limit_bytes=32 << 20),
        cost_estimate=pl.CostEstimate(
            flops=800_000_000, bytes_accessed=4 << 20, transcendentals=0
        ),
        name="convolve",
    )(there, past, spec, freq, skip, into_lo, cols_in, cols_out, back, twist)


def output_kernel(conv_ref, query_ref, w_ref, out_hbm, out_ref, sems):
    rows = query_ref.shape[0] // PIECES
    copies = []
    for piece in range(PIECES):
        at = slice(piece * rows, (piece + 1) * rows)
        conv = jnp.transpose(conv_ref[:, at].astype(jnp.float32), (1, 0))
        gated = (query_ref[at] * conv).astype(jnp.bfloat16)
        out_ref[at] = dot(gated, w_ref[...]).astype(jnp.bfloat16)
        copies.append(pltpu.make_async_copy(out_ref.at[at], out_hbm.at[at], sems.at[piece]))
        copies[-1].start()
    for copy in copies:
        copy.wait()


def project_out(conv, query, w_out):
    rows = query.shape[0]
    return pl.pallas_call(
        output_kernel,
        out_shape=jax.ShapeDtypeStruct((rows, D), jnp.bfloat16),
        in_specs=[VMEM] * 3,
        out_specs=HBM,
        scratch_shapes=[
            pltpu.VMEM((rows, D), jnp.bfloat16), pltpu.SemaphoreType.DMA((PIECES,))
        ],
        compiler_params=pltpu.CompilerParams(vmem_limit_bytes=16 << 20),
        cost_estimate=pl.CostEstimate(
            flops=2 * rows * D * D, bytes_accessed=2 << 20, transcendentals=0
        ),
        name="project_out",
    )(conv, query, w_out)


def rotated(array, axes):
    count = lax.axis_size(axes)
    return lax.ppermute(array, axes, [(i, (i + 1) % count) for i in range(count)])


def per_device(tokens, w_in, short_filter, long_filter, skip_gain, w_out):
    rows = tokens.shape[0]
    peers = lax.axis_size("tok")
    into_lo, into_hi, cols_in, cols_wide, cols_out, back, twist = dft_tables()
    span = lax.axis_index("span")
    there = jnp.stack([span + lax.axis_index("tok") > 0, span > 0]).astype(jnp.float32)
    there = jnp.broadcast_to(there[:, None], (2, D))
    rim = rotated(tokens[rows - RIM :], ("span", "tok"))
    product, head, w_part, taps = project(tokens, w_in, short_filter)
    product = fix_rim(there, rim, w_part, taps, head, product)
    own = lax.all_to_all(
        product.reshape(peers, D // peers, rows), "tok", split_axis=0, concat_axis=0, tiled=True
    )
    past = rotated(own, "span")
    spec, freq, skip = early(long_filter, own, skip_gain.reshape(-1, 1), into_lo, into_hi, cols_wide, twist)
    query = make_query(there, tokens, rim, w_in, short_filter)
    freq, query = lax.optimization_barrier((freq, query))
    conv = convolve(there, past, spec, freq, skip, into_lo, cols_in, cols_out, back, twist)
    conv = lax.all_to_all(conv, "tok", split_axis=0, concat_axis=0, tiled=True)
    return project_out(conv.reshape(D, rows), query, w_out)


def solution(mesh):
    return jax.shard_map(
        per_device,
        mesh=mesh,
        in_specs=(P(("span", "tok"), None), P(), P(), P("tok", None), P("tok"), P()),
        out_specs=P(("span", "tok"), None),
        check_vma=False,
    )
```

```python
import jax
import jax.numpy as jnp
import numpy as np
from jax import lax
from jax.experimental import pallas as pl
from jax.experimental.pallas import tpu as pltpu
from jax.sharding import PartitionSpec as P

D = 256
LANES = 128
HALF = 64
RIM = 16
POINTS = LANES * LANES


def dft_tables():
    ka = np.arange(HALF) + 0.5
    idx = np.arange(LANES)
    wave = lambda phase: np.exp(-2j * np.pi * phase)
    rows = wave(np.outer(ka, idx) / LANES)
    twist = wave(np.outer(ka, idx) / POINTS)
    cols = wave(np.outer(idx, idx) / LANES)
    into = np.concatenate([rows.real, rows.imag], 0)
    back = into.T[HALF:] * (2.0 / POINTS)
    cols_in = np.block([[cols.real, cols.imag], [-cols.imag, cols.real]])
    cols_out = np.block([[cols.real.T, -cols.imag.T], [cols.imag.T, cols.real.T]])
    bf = lambda a: a.astype(np.float32).astype(jnp.bfloat16)
    pair = lambda a: np.concatenate([bf(a), bf(a - bf(a).astype(np.float64))], 1)
    twist = np.stack([twist.real, twist.imag]).astype(np.float32)
    high = bf(cols_in)
    wide = np.concatenate([high, bf(cols_in - high.astype(np.float64)), high], 0)
    tables = pair(into[:, :HALF]), pair(into), high, wide, bf(cols_out), pair(back), twist
    return [jnp.asarray(table) for table in tables]


def dot(a, b):
    return jnp.dot(a, b, preferred_element_type=jnp.float32)


VMEM = pl.BlockSpec(memory_space=pltpu.VMEM)
HBM = pl.BlockSpec(memory_space=pltpu.MemorySpace.HBM)
HEAD = 8
PIECES = 2


def short_filter_sum(taps, now, one, two):
    return taps[0:1] * now + taps[1:2] * one + taps[2:3] * two


def rounded(projected):
    return projected.astype(jnp.bfloat16).astype(jnp.float32)


def project_kernel(
    tokens_hbm, w_hbm, taps_hbm, product_ref, head_ref, w_ref, taps_ref, tokens_ref, sems
):
    copies = [
        pltpu.make_async_copy(w_hbm.at[:, pl.ds(D, 2 * D)], w_ref, sems.at[0]),
        pltpu.make_async_copy(tokens_hbm, tokens_ref, sems.at[1]),
        pltpu.make_async_copy(taps_hbm, taps_ref, sems.at[2]),
    ]
    for copy in copies:
        copy.start()
    for copy in copies:
        copy.wait()

    now = rounded(dot(tokens_ref[...], w_ref[...]))
    head_ref[...] = now[:HEAD]
    mixed = short_filter_sum(
        taps_ref[:, D:], now, pltpu.roll(now, 1, axis=0), pltpu.roll(now, 2, axis=0)
    )
    product = mixed[:, :D] * mixed[:, D:]
    product_ref[...] = jnp.transpose(product, (1, 0)).astype(jnp.bfloat16)


def project(tokens, w_in, short_filter):
    rows = tokens.shape[0]
    inputs = [
        pltpu.with_memory_space_constraint(a, pltpu.MemorySpace.HBM)
        for a in (tokens, w_in, short_filter)
    ]
    return pl.pallas_call(
        project_kernel,
        out_shape=(
            jax.ShapeDtypeStruct((D, rows), jnp.bfloat16),
            jax.ShapeDtypeStruct((HEAD, 2 * D), jnp.float32),
            jax.ShapeDtypeStruct((D, 2 * D), w_in.dtype),
            jax.ShapeDtypeStruct(short_filter.shape, short_filter.dtype),
        ),
        in_specs=[HBM] * 3,
        out_specs=(VMEM,) * 4,
        scratch_shapes=[pltpu.VMEM(tokens.shape, tokens.dtype), pltpu.SemaphoreType.DMA((3,))],
        compiler_params=pltpu.CompilerParams(vmem_limit_bytes=24 << 20),
        cost_estimate=pl.CostEstimate(
            flops=2 * rows * D * 2 * D, bytes_accessed=2 << 20, transcendentals=0
        ),
        name="project",
    )(*inputs)


def rim_kernel(there_ref, rim_ref, w_ref, taps_ref, head_ref, raw_ref, product_ref):
    before = rounded(dot(rim_ref[...], w_ref[...]))[RIM - HEAD :]
    there = jnp.concatenate([there_ref[0:1], there_ref[0:1]], axis=1)
    before = jnp.where(there > 0.0, before, 0.0)
    both = jnp.concatenate([before, head_ref[...]], axis=0)
    mixed = short_filter_sum(
        taps_ref[:, D:], both, pltpu.roll(both, 1, axis=0), pltpu.roll(both, 2, axis=0)
    )[HEAD:]
    fixed = mixed[:, :D] * mixed[:, D:]
    fixed = jnp.concatenate([fixed, jnp.zeros((LANES - HEAD, D), jnp.float32)], axis=0)
    fixed = jnp.transpose(fixed, (1, 0)).astype(jnp.bfloat16)
    lane = lax.broadcasted_iota(jnp.int32, fixed.shape, 1)
    product_ref[:, LANES:] = raw_ref[:, LANES:]
    product_ref[:, :LANES] = jnp.where(lane < HEAD, fixed, raw_ref[:, :LANES])


def fix_rim(there, rim, w_part, short_filter, head, product):
    return pl.pallas_call(
        rim_kernel,
        out_shape=jax.ShapeDtypeStruct(product.shape, product.dtype),
        in_specs=[VMEM] * 6,
        out_specs=VMEM,
        compiler_params=pltpu.CompilerParams(vmem_limit_bytes=16 << 20),
        cost_estimate=pl.CostEstimate(flops=20_000_000, bytes_accessed=1 << 20, transcendentals=0),
        name="fix_rim",
    )(there, rim, w_part, short_filter, head, product)


def query_kernel(there_ref, tokens_ref, rim_ref, w_ref, taps_ref, query_ref):
    weights = w_ref[:, :D]
    taps = taps_ref[:, :D]
    now = rounded(dot(tokens_ref[...], weights))
    query_ref[...] = short_filter_sum(
        taps, now, pltpu.roll(now, 1, axis=0), pltpu.roll(now, 2, axis=0)
    )
    before = rounded(dot(rim_ref[...], weights))[RIM - HEAD :]
    both = jnp.concatenate([jnp.where(there_ref[0:1] > 0.0, before, 0.0), now[:HEAD]], axis=0)
    query_ref[:HEAD] = short_filter_sum(
        taps, both, pltpu.roll(both, 1, axis=0), pltpu.roll(both, 2, axis=0)
    )[HEAD:]


def make_query(there, tokens, rim, w_in, short_filter):
    rows = tokens.shape[0]
    return pl.pallas_call(
        query_kernel,
        out_shape=jax.ShapeDtypeStruct((rows, D), jnp.float32),
        in_specs=[VMEM] * 5,
        out_specs=VMEM,
        compiler_params=pltpu.CompilerParams(vmem_limit_bytes=16 << 20),
        cost_estimate=pl.CostEstimate(
            flops=2 * rows * D * D, bytes_accessed=1 << 20, transcendentals=0
        ),
        name="make_query",
    )(there, tokens, rim, w_in, short_filter)


def put_rows(load, scratch, chans, tiles, at):
    for tile in range(tiles):
        scratch[pl.ds((at + tile) * chans, chans), :] = load(tile).astype(jnp.float32)


def by_channel(scratch, chans, at, tiles):
    return jnp.concatenate(
        [scratch[pl.ds(at * chans + c, tiles, stride=chans), :] for c in range(chans)], axis=1
    )


def forward(into, cols_in, twist_re, twist_im, data, chans):
    parts = cols_in.shape[0] // (2 * LANES)
    first = dot(into, jnp.concatenate([data, data], axis=0))
    spun = []
    for c in range(chans):
        re = first[:HALF, c * LANES : (c + 1) * LANES]
        im = first[HALF:, c * LANES : (c + 1) * LANES]
        turned = jnp.concatenate(
            [re * twist_re - im * twist_im, re * twist_im + im * twist_re], axis=1
        )
        high = turned.astype(jnp.bfloat16)
        row = [high] * min(parts, 2)
        if parts == 3:
            row.append((turned - high.astype(jnp.float32)).astype(jnp.bfloat16))
        spun.append(jnp.concatenate(row, axis=1) if parts > 1 else high)
    return dot(jnp.concatenate(spun, axis=0), cols_in)


def rows_of(ref):
    per = ref.shape[2] // LANES
    return lambda i: ref[i // per, :, (i % per) * LANES : (i % per + 1) * LANES]


def early_kernel(
    filter_ref, own_ref, gain_ref, into_lo_ref, cols_in_ref, twist_ref, spec_ref,
    data_ref, skip_ref, rows_ref,
):
    chans, taps = filter_ref.shape
    tiles = taps // LANES
    put_rows(lambda i: filter_ref[:, i * LANES : (i + 1) * LANES], rows_ref, chans, tiles, 0)
    gain = jnp.broadcast_to(gain_ref[...], (chans, LANES))
    per = own_ref.shape[2] // LANES
    for tile in range(tiles):
        lanes = slice(tile % per * LANES, (tile % per + 1) * LANES)
        own = own_ref[tile // per, :, lanes].astype(jnp.float32)
        rows_ref[pl.ds((tiles + tile) * chans, chans), :] = own
        skip_ref[tile // per, :, lanes] = gain * own
    twist = twist_ref[0], twist_ref[1]
    data = by_channel(rows_ref, chans, 0, tiles).astype(jnp.bfloat16)
    spec_ref[...] = forward(into_lo_ref[...], cols_in_ref[...], *twist, data, chans)
    data = by_channel(rows_ref, chans, tiles, tiles)
    data_ref[...] = data.astype(jnp.bfloat16)


def early(long_filter, own, gain, into_lo, cols_in, twist):
    chans, taps = long_filter.shape
    tiles = taps // LANES
    points = jax.ShapeDtypeStruct((chans * HALF, 2 * LANES), jnp.float32)
    return pl.pallas_call(
        early_kernel,
        out_shape=(
            points,
            jax.ShapeDtypeStruct((tiles, chans * LANES), jnp.bfloat16),
            jax.ShapeDtypeStruct(own.shape, jnp.float32),
        ),
        in_specs=[VMEM] * 6,
        out_specs=(VMEM,) * 3,
        scratch_shapes=[pltpu.VMEM((2 * tiles * chans, LANES), jnp.float32)],
        compiler_params=pltpu.CompilerParams(vmem_limit_bytes=24 << 20),
        cost_estimate=pl.CostEstimate(
            flops=800_000_000, bytes_accessed=3 << 20, transcendentals=0
        ),
        name="early",
    )(long_filter, own, gain, into_lo, cols_in, twist)


def convolve_kernel(
    there_ref, past_ref, spec_ref, data_ref, skip_ref, into_ref, cols_in_ref, cols_out_ref,
    back_ref, twist_ref, out_ref, rows_ref,
):
    peers, chans, width = out_ref.shape
    per = width // LANES
    tiles = peers * per
    twist_re = twist_ref[0]
    twist_im = twist_ref[1]
    there = jnp.broadcast_to(there_ref[1:2, :LANES], (chans, LANES)) > 0.0
    load = rows_of(past_ref)
    put_rows(lambda i: jnp.where(there, load(i).astype(jnp.float32), 0.0), rows_ref, chans, tiles, 0)
    past = by_channel(rows_ref, chans, 0, tiles).astype(jnp.bfloat16)
    data = jnp.concatenate([past, data_ref[...]], axis=0)
    freq = forward(into_ref[...], cols_in_ref[...], twist_re, twist_im, data, chans)
    spec = spec_ref[...]
    fre, fim = freq[:, :LANES], freq[:, LANES:]
    sre, sim = spec[:, :LANES], spec[:, LANES:]
    prod = jnp.concatenate([fre * sre - fim * sim, fre * sim + fim * sre], axis=1)
    last = dot(prod.astype(jnp.bfloat16), cols_out_ref[...])
    spun = []
    for c in range(chans):
        re = last[c * HALF : (c + 1) * HALF, :LANES]
        im = last[c * HALF : (c + 1) * HALF, LANES:]
        spun.append(
            jnp.concatenate(
                [re * twist_re + im * twist_im, im * twist_re - re * twist_im], axis=0
            ).astype(jnp.bfloat16)
        )
    spun = jnp.concatenate(spun, axis=1)
    result = dot(back_ref[...], jnp.concatenate([spun, spun], axis=0))
    for c in range(chans):
        lanes = slice(c * LANES, (c + 1) * LANES)
        rows_ref[pl.ds(c, tiles, stride=chans), :] = result[:, lanes]
    for tile in range(tiles):
        lanes = slice(tile % per * LANES, (tile % per + 1) * LANES)
        out = rows_ref[pl.ds(tile * chans, chans), :] + skip_ref[tile // per, :, lanes]
        out_ref[tile // per, :, lanes] = out.astype(jnp.bfloat16)


def convolve(there, past, spec, data, skip, into, cols_in, cols_out, back, twist):
    peers, chans, width = past.shape
    return pl.pallas_call(
        convolve_kernel,
        out_shape=jax.ShapeDtypeStruct(past.shape, jnp.bfloat16),
        in_specs=[VMEM] * 10,
        out_specs=VMEM,
        scratch_shapes=[pltpu.VMEM((peers * chans * width // LANES, LANES), jnp.float32)],
        compiler_params=pltpu.CompilerParams(vmem_limit_bytes=32 << 20),
        cost_estimate=pl.CostEstimate(
            flops=800_000_000, bytes_accessed=4 << 20, transcendentals=0
        ),
        name="convolve",
    )(there, past, spec, data, skip, into, cols_in, cols_out, back, twist)


def output_kernel(conv_ref, query_ref, w_ref, out_hbm, out_ref, sems):
    rows = query_ref.shape[0] // PIECES
    copies = []
    for piece in range(PIECES):
        at = slice(piece * rows, (piece + 1) * rows)
        conv = jnp.transpose(conv_ref[:, at].astype(jnp.float32), (1, 0))
        gated = (query_ref[at] * conv).astype(jnp.bfloat16)
        out_ref[at] = dot(gated, w_ref[...]).astype(jnp.bfloat16)
        copies.append(pltpu.make_async_copy(out_ref.at[at], out_hbm.at[at], sems.at[piece]))
        copies[-1].start()
    for copy in copies:
        copy.wait()


def project_out(conv, query, w_out):
    rows = query.shape[0]
    return pl.pallas_call(
        output_kernel,
        out_shape=jax.ShapeDtypeStruct((rows, D), jnp.bfloat16),
        in_specs=[VMEM] * 3,
        out_specs=HBM,
        scratch_shapes=[
            pltpu.VMEM((rows, D), jnp.bfloat16), pltpu.SemaphoreType.DMA((PIECES,))
        ],
        compiler_params=pltpu.CompilerParams(vmem_limit_bytes=16 << 20),
        cost_estimate=pl.CostEstimate(
            flops=2 * rows * D * D, bytes_accessed=2 << 20, transcendentals=0
        ),
        name="project_out",
    )(conv, query, w_out)


def rotated(array, axes):
    count = lax.axis_size(axes)
    return lax.ppermute(array, axes, [(i, (i + 1) % count) for i in range(count)])


def per_device(tokens, w_in, short_filter, long_filter, skip_gain, w_out):
    rows = tokens.shape[0]
    peers = lax.axis_size("tok")
    into_lo, into, cols_in, cols_wide, cols_out, back, twist = dft_tables()
    span = lax.axis_index("span")
    there = jnp.stack([span + lax.axis_index("tok") > 0, span > 0]).astype(jnp.float32)
    there = jnp.broadcast_to(there[:, None], (2, D))
    rim = rotated(tokens[rows - RIM :], ("span", "tok"))
    product, head, w_part, taps = project(tokens, w_in, short_filter)
    product = fix_rim(there, rim, w_part, taps, head, product)
    own = lax.all_to_all(
        product.reshape(peers, D // peers, rows), "tok", split_axis=0, concat_axis=0, tiled=True
    )
    past = rotated(own, "span")
    spec, data, skip = early(
        long_filter, own, skip_gain.reshape(-1, 1), into_lo, cols_wide, twist
    )
    query = make_query(there, tokens, rim, w_in, short_filter)
    data, query = lax.optimization_barrier((data, query))
    conv = convolve(there, past, spec, data, skip, into, cols_in, cols_out, back, twist)
    conv = lax.all_to_all(conv, "tok", split_axis=0, concat_axis=0, tiled=True)
    return project_out(conv.reshape(D, rows), query, w_out)


def solution(mesh):
    return jax.shard_map(
        per_device,
        mesh=mesh,
        in_specs=(P(("span", "tok"), None), P(), P(), P("tok", None), P("tok"), P()),
        out_specs=P(("span", "tok"), None),
        check_vma=False,
    )
```

```python
import jax
import jax.numpy as jnp
import numpy as np
from jax import lax
from jax.experimental import pallas as pl
from jax.experimental.pallas import tpu as pltpu
from jax.sharding import PartitionSpec as P

D = 256
LANES = 128
HALF = 64
RIM = 16
POINTS = LANES * LANES


def dft_tables():
    ka = np.arange(HALF) + 0.5
    idx = np.arange(LANES)
    wave = lambda phase: np.exp(-2j * np.pi * phase)
    rows = wave(np.outer(ka, idx) / LANES)
    twist = wave(np.outer(ka, idx) / POINTS)
    cols = wave(np.outer(idx, idx) / LANES)
    into = np.concatenate([rows.real, rows.imag], 0)
    back = into.T[HALF:] * (2.0 / POINTS)
    cols_in = np.block([[cols.real, cols.imag], [-cols.imag, cols.real]])
    cols_out = np.block([[cols.real.T, -cols.imag.T], [cols.imag.T, cols.real.T]])
    bf = lambda a: a.astype(np.float32).astype(jnp.bfloat16)
    pair = lambda a: np.concatenate([bf(a), bf(a - bf(a).astype(np.float64))], 1)
    twist = np.stack([twist.real, twist.imag]).astype(np.float32)
    high = bf(cols_in)
    wide = np.concatenate([high, bf(cols_in - high.astype(np.float64)), high], 0)
    tables = pair(into[:, :HALF]), pair(into[:, HALF:]), high, wide, bf(cols_out), pair(back), twist
    return [jnp.asarray(table) for table in tables]


def dot(a, b):
    return jnp.dot(a, b, preferred_element_type=jnp.float32)


VMEM = pl.BlockSpec(memory_space=pltpu.VMEM)
HBM = pl.BlockSpec(memory_space=pltpu.MemorySpace.HBM)
HEAD = 8
PIECES = 2


def short_filter_sum(taps, now, one, two):
    return taps[0:1] * now + taps[1:2] * one + taps[2:3] * two


def rounded(projected):
    return projected.astype(jnp.bfloat16).astype(jnp.float32)


def project_kernel(
    tokens_hbm, w_hbm, taps_hbm, product_ref, head_ref, w_ref, taps_ref, tokens_ref, sems
):
    copies = [
        pltpu.make_async_copy(w_hbm.at[:, pl.ds(D, 2 * D)], w_ref, sems.at[0]),
        pltpu.make_async_copy(tokens_hbm, tokens_ref, sems.at[1]),
        pltpu.make_async_copy(taps_hbm, taps_ref, sems.at[2]),
    ]
    for copy in copies:
        copy.start()
    for copy in copies:
        copy.wait()

    now = rounded(dot(tokens_ref[...], w_ref[...]))
    head_ref[...] = now[:HEAD]
    mixed = short_filter_sum(
        taps_ref[:, D:], now, pltpu.roll(now, 1, axis=0), pltpu.roll(now, 2, axis=0)
    )
    product = mixed[:, :D] * mixed[:, D:]
    product_ref[...] = jnp.transpose(product, (1, 0)).astype(jnp.bfloat16)


def project(tokens, w_in, short_filter):
    rows = tokens.shape[0]
    inputs = [
        pltpu.with_memory_space_constraint(a, pltpu.MemorySpace.HBM)
        for a in (tokens, w_in, short_filter)
    ]
    return pl.pallas_call(
        project_kernel,
        out_shape=(
            jax.ShapeDtypeStruct((D, rows), jnp.bfloat16),
            jax.ShapeDtypeStruct((HEAD, 2 * D), jnp.float32),
            jax.ShapeDtypeStruct((D, 2 * D), w_in.dtype),
            jax.ShapeDtypeStruct(short_filter.shape, short_filter.dtype),
        ),
        in_specs=[HBM] * 3,
        out_specs=(VMEM,) * 4,
        scratch_shapes=[pltpu.VMEM(tokens.shape, tokens.dtype), pltpu.SemaphoreType.DMA((3,))],
        compiler_params=pltpu.CompilerParams(vmem_limit_bytes=24 << 20),
        cost_estimate=pl.CostEstimate(
            flops=2 * rows * D * 2 * D, bytes_accessed=2 << 20, transcendentals=0
        ),
        name="project",
    )(*inputs)


def rim_kernel(there_ref, rim_ref, w_ref, taps_ref, head_ref, raw_ref, product_ref):
    before = rounded(dot(rim_ref[...], w_ref[...]))[RIM - HEAD :]
    there = jnp.concatenate([there_ref[0:1], there_ref[0:1]], axis=1)
    before = jnp.where(there > 0.0, before, 0.0)
    both = jnp.concatenate([before, head_ref[...]], axis=0)
    mixed = short_filter_sum(
        taps_ref[:, D:], both, pltpu.roll(both, 1, axis=0), pltpu.roll(both, 2, axis=0)
    )[HEAD:]
    fixed = mixed[:, :D] * mixed[:, D:]
    fixed = jnp.concatenate([fixed, jnp.zeros((LANES - HEAD, D), jnp.float32)], axis=0)
    fixed = jnp.transpose(fixed, (1, 0)).astype(jnp.bfloat16)
    lane = lax.broadcasted_iota(jnp.int32, fixed.shape, 1)
    product_ref[:, LANES:] = raw_ref[:, LANES:]
    product_ref[:, :LANES] = jnp.where(lane < HEAD, fixed, raw_ref[:, :LANES])


def fix_rim(there, rim, w_part, short_filter, head, product):
    return pl.pallas_call(
        rim_kernel,
        out_shape=jax.ShapeDtypeStruct(product.shape, product.dtype),
        in_specs=[VMEM] * 6,
        out_specs=VMEM,
        compiler_params=pltpu.CompilerParams(vmem_limit_bytes=16 << 20),
        cost_estimate=pl.CostEstimate(flops=20_000_000, bytes_accessed=1 << 20, transcendentals=0),
        name="fix_rim",
    )(there, rim, w_part, short_filter, head, product)


def query_kernel(there_ref, tokens_ref, rim_ref, w_ref, taps_ref, query_ref):
    weights = w_ref[:, :D]
    taps = taps_ref[:, :D]
    now = rounded(dot(tokens_ref[...], weights))
    query_ref[...] = short_filter_sum(
        taps, now, pltpu.roll(now, 1, axis=0), pltpu.roll(now, 2, axis=0)
    )
    before = rounded(dot(rim_ref[...], weights))[RIM - HEAD :]
    both = jnp.concatenate([jnp.where(there_ref[0:1] > 0.0, before, 0.0), now[:HEAD]], axis=0)
    query_ref[:HEAD] = short_filter_sum(
        taps, both, pltpu.roll(both, 1, axis=0), pltpu.roll(both, 2, axis=0)
    )[HEAD:]


def make_query(there, tokens, rim, w_in, short_filter):
    rows = tokens.shape[0]
    return pl.pallas_call(
        query_kernel,
        out_shape=jax.ShapeDtypeStruct((rows, D), jnp.float32),
        in_specs=[VMEM] * 5,
        out_specs=VMEM,
        compiler_params=pltpu.CompilerParams(vmem_limit_bytes=16 << 20),
        cost_estimate=pl.CostEstimate(
            flops=2 * rows * D * D, bytes_accessed=1 << 20, transcendentals=0
        ),
        name="make_query",
    )(there, tokens, rim, w_in, short_filter)


def put_rows(load, scratch, chans, tiles, at):
    for tile in range(tiles):
        scratch[pl.ds((at + tile) * chans, chans), :] = load(tile).astype(jnp.float32)


def by_channel(scratch, chans, at, tiles):
    return jnp.concatenate(
        [scratch[pl.ds(at * chans + c, tiles, stride=chans), :] for c in range(chans)], axis=1
    )


def forward(into, cols_in, twist_re, twist_im, data, chans):
    parts = cols_in.shape[0] // (2 * LANES)
    first = dot(into, jnp.concatenate([data, data], axis=0))
    spun = []
    for c in range(chans):
        re = first[:HALF, c * LANES : (c + 1) * LANES]
        im = first[HALF:, c * LANES : (c + 1) * LANES]
        turned = jnp.concatenate(
            [re * twist_re - im * twist_im, re * twist_im + im * twist_re], axis=1
        )
        high = turned.astype(jnp.bfloat16)
        row = [high] * min(parts, 2)
        if parts == 3:
            row.append((turned - high.astype(jnp.float32)).astype(jnp.bfloat16))
        spun.append(jnp.concatenate(row, axis=1) if parts > 1 else high)
    return dot(jnp.concatenate(spun, axis=0), cols_in)


def rows_of(ref):
    per = ref.shape[2] // LANES
    return lambda i: ref[i // per, :, (i % per) * LANES : (i % per + 1) * LANES]


def early_kernel(
    filter_ref, own_ref, gain_ref, into_lo_ref, into_hi_ref, cols_in_ref, twist_ref, spec_ref,
    freq_ref, skip_ref, rows_ref,
):
    chans, taps = filter_ref.shape
    tiles = taps // LANES
    put_rows(lambda i: filter_ref[:, i * LANES : (i + 1) * LANES], rows_ref, chans, tiles, 0)
    gain = jnp.broadcast_to(gain_ref[...], (chans, LANES))
    per = own_ref.shape[2] // LANES
    for tile in range(tiles):
        lanes = slice(tile % per * LANES, (tile % per + 1) * LANES)
        own = own_ref[tile // per, :, lanes].astype(jnp.float32)
        rows_ref[pl.ds((tiles + tile) * chans, chans), :] = own
        skip_ref[tile // per, :, lanes] = gain * own
    twist = twist_ref[0], twist_ref[1]
    data = by_channel(rows_ref, chans, 0, tiles).astype(jnp.bfloat16)
    spec_ref[...] = forward(into_lo_ref[...], cols_in_ref[...], *twist, data, chans)
    data = by_channel(rows_ref, chans, tiles, tiles)
    freq_ref[...] = forward(
        into_hi_ref[...], cols_in_ref[: 4 * LANES], *twist, data.astype(jnp.bfloat16), chans
    )


def early(long_filter, own, gain, into_lo, into_hi, cols_in, twist):
    chans, taps = long_filter.shape
    tiles = taps // LANES
    points = jax.ShapeDtypeStruct((chans * HALF, 2 * LANES), jnp.float32)
    return pl.pallas_call(
        early_kernel,
        out_shape=(points, points, jax.ShapeDtypeStruct(own.shape, jnp.float32)),
        in_specs=[VMEM] * 7,
        out_specs=(VMEM,) * 3,
        scratch_shapes=[pltpu.VMEM((2 * tiles * chans, LANES), jnp.float32)],
        compiler_params=pltpu.CompilerParams(vmem_limit_bytes=24 << 20),
        cost_estimate=pl.CostEstimate(
            flops=800_000_000, bytes_accessed=3 << 20, transcendentals=0
        ),
        name="early",
    )(long_filter, own, gain, into_lo, into_hi, cols_in, twist)


def convolve_kernel(
    there_ref, past_ref, spec_ref, freq_ref, skip_ref, into_lo_ref, cols_in_ref, cols_out_ref,
    back_ref, twist_ref, out_ref, rows_ref,
):
    peers, chans, width = out_ref.shape
    per = width // LANES
    tiles = peers * per
    twist_re = twist_ref[0]
    twist_im = twist_ref[1]
    there = jnp.broadcast_to(there_ref[1:2, :LANES], (chans, LANES)) > 0.0
    load = rows_of(past_ref)
    put_rows(lambda i: jnp.where(there, load(i).astype(jnp.float32), 0.0), rows_ref, chans, tiles, 0)
    past = by_channel(rows_ref, chans, 0, tiles).astype(jnp.bfloat16)
    freq = forward(into_lo_ref[...], cols_in_ref[...], twist_re, twist_im, past, chans) + freq_ref[...]
    spec = spec_ref[...]
    fre, fim = freq[:, :LANES], freq[:, LANES:]
    sre, sim = spec[:, :LANES], spec[:, LANES:]
    prod = jnp.concatenate([fre * sre - fim * sim, fre * sim + fim * sre], axis=1)
    last = dot(prod.astype(jnp.bfloat16), cols_out_ref[...])
    spun = []
    for c in range(chans):
        re = last[c * HALF : (c + 1) * HALF, :LANES]
        im = last[c * HALF : (c + 1) * HALF, LANES:]
        spun.append(
            jnp.concatenate(
                [re * twist_re + im * twist_im, im * twist_re - re * twist_im], axis=0
            ).astype(jnp.bfloat16)
        )
    spun = jnp.concatenate(spun, axis=1)
    result = dot(back_ref[...], jnp.concatenate([spun, spun], axis=0))
    for c in range(chans):
        lanes = slice(c * LANES, (c + 1) * LANES)
        rows_ref[pl.ds(c, tiles, stride=chans), :] = result[:, lanes]
    for tile in range(tiles):
        lanes = slice(tile % per * LANES, (tile % per + 1) * LANES)
        out = rows_ref[pl.ds(tile * chans, chans), :] + skip_ref[tile // per, :, lanes]
        out_ref[tile // per, :, lanes] = out.astype(jnp.bfloat16)


def convolve(there, past, spec, freq, skip, into_lo, cols_in, cols_out, back, twist):
    peers, chans, width = past.shape
    return pl.pallas_call(
        convolve_kernel,
        out_shape=jax.ShapeDtypeStruct(past.shape, jnp.bfloat16),
        in_specs=[VMEM] * 10,
        out_specs=VMEM,
        scratch_shapes=[pltpu.VMEM((peers * chans * width // LANES, LANES), jnp.float32)],
        compiler_params=pltpu.CompilerParams(vmem_limit_bytes=32 << 20),
        cost_estimate=pl.CostEstimate(
            flops=800_000_000, bytes_accessed=4 << 20, transcendentals=0
        ),
        name="convolve",
    )(there, past, spec, freq, skip, into_lo, cols_in, cols_out, back, twist)


def output_kernel(conv_ref, query_ref, w_ref, out_hbm, out_ref, sems):
    rows = query_ref.shape[0] // PIECES
    copies = []
    for piece in range(PIECES):
        at = slice(piece * rows, (piece + 1) * rows)
        conv = jnp.transpose(conv_ref[:, at].astype(jnp.float32), (1, 0))
        gated = (query_ref[at] * conv).astype(jnp.bfloat16)
        out_ref[at] = dot(gated, w_ref[...]).astype(jnp.bfloat16)
        copies.append(pltpu.make_async_copy(out_ref.at[at], out_hbm.at[at], sems.at[piece]))
        copies[-1].start()
    for copy in copies:
        copy.wait()


def project_out(conv, query, w_out):
    rows = query.shape[0]
    return pl.pallas_call(
        output_kernel,
        out_shape=jax.ShapeDtypeStruct((rows, D), jnp.bfloat16),
        in_specs=[VMEM] * 3,
        out_specs=HBM,
        scratch_shapes=[
            pltpu.VMEM((rows, D), jnp.bfloat16), pltpu.SemaphoreType.DMA((PIECES,))
        ],
        compiler_params=pltpu.CompilerParams(vmem_limit_bytes=16 << 20),
        cost_estimate=pl.CostEstimate(
            flops=2 * rows * D * D, bytes_accessed=2 << 20, transcendentals=0
        ),
        name="project_out",
    )(conv, query, w_out)


def rotated(array, axes):
    count = lax.axis_size(axes)
    return lax.ppermute(array, axes, [(i, (i + 1) % count) for i in range(count)])


def per_device(tokens, w_in, short_filter, long_filter, skip_gain, w_out):
    rows = tokens.shape[0]
    peers = lax.axis_size("tok")
    into_lo, into_hi, cols_in, cols_wide, cols_out, back, twist = dft_tables()
    span = lax.axis_index("span")
    there = jnp.stack([span + lax.axis_index("tok") > 0, span > 0]).astype(jnp.float32)
    there = jnp.broadcast_to(there[:, None], (2, D))
    w_in, there = lax.optimization_barrier((w_in, there))
    rim = rotated(tokens[rows - RIM :], ("span", "tok"))
    product, head, w_part, taps = project(tokens, w_in, short_filter)
    head, there, rim = lax.optimization_barrier((head, there, rim))
    product = fix_rim(there, rim, w_part, taps, head, product)
    own = lax.all_to_all(
        product.reshape(peers, D // peers, rows), "tok", split_axis=0, concat_axis=0, tiled=True
    )
    past = rotated(own, "span")
    spec, freq, skip = early(long_filter, own, skip_gain.reshape(-1, 1), into_lo, into_hi, cols_wide, twist)
    query = make_query(there, tokens, rim, w_in, short_filter)
    freq, query = lax.optimization_barrier((freq, query))
    conv = convolve(there, past, spec, freq, skip, into_lo, cols_in, cols_out, back, twist)
    conv = lax.all_to_all(conv, "tok", split_axis=0, concat_axis=0, tiled=True)
    return project_out(conv.reshape(D, rows), query, w_out)


def solution(mesh):
    return jax.shard_map(
        per_device,
        mesh=mesh,
        in_specs=(P(("span", "tok"), None), P(), P(), P("tok", None), P("tok"), P()),
        out_specs=P(("span", "tok"), None),
        check_vma=False,
    )
```

```python
import jax
import jax.numpy as jnp
import numpy as np
from jax import lax
from jax.experimental import pallas as pl
from jax.experimental.pallas import tpu as pltpu
from jax.sharding import PartitionSpec as P

D = 256
LANES = 128
HALF = 64
RIM = 16
POINTS = LANES * LANES


def dft_tables():
    ka = np.arange(HALF) + 0.5
    idx = np.arange(LANES)
    wave = lambda phase: np.exp(-2j * np.pi * phase)
    rows = wave(np.outer(ka, idx) / LANES)
    twist = wave(np.outer(ka, idx) / POINTS)
    cols = wave(np.outer(idx, idx) / LANES)
    into = np.concatenate([rows.real, rows.imag], 0)
    back = into.T[HALF:] * (2.0 / POINTS)
    cols_in = np.block([[cols.real, cols.imag], [-cols.imag, cols.real]])
    cols_out = np.block([[cols.real.T, -cols.imag.T], [cols.imag.T, cols.real.T]])
    bf = lambda a: a.astype(np.float32).astype(jnp.bfloat16)
    pair = lambda a: np.concatenate([bf(a), bf(a - bf(a).astype(np.float64))], 1)
    twist = np.stack([twist.real, twist.imag]).astype(np.float32)
    high = bf(cols_in)
    wide = np.concatenate([high, bf(cols_in - high.astype(np.float64)), high], 0)
    tables = pair(into[:, :HALF]), pair(into[:, HALF:]), high, wide, bf(cols_out), pair(back), twist
    return [jnp.asarray(table) for table in tables]


def dot(a, b):
    return jnp.dot(a, b, preferred_element_type=jnp.float32)


VMEM = pl.BlockSpec(memory_space=pltpu.VMEM)
HBM = pl.BlockSpec(memory_space=pltpu.MemorySpace.HBM)
HEAD = 8
PIECES = 4


def short_filter_sum(taps, now, one, two):
    return taps[0:1] * now + taps[1:2] * one + taps[2:3] * two


def rounded(projected):
    return projected.astype(jnp.bfloat16).astype(jnp.float32)


def project_kernel(
    tokens_hbm, w_hbm, taps_hbm, product_ref, head_ref, w_ref, taps_ref, tokens_ref, sems
):
    copies = [
        pltpu.make_async_copy(w_hbm.at[:, pl.ds(D, 2 * D)], w_ref, sems.at[0]),
        pltpu.make_async_copy(tokens_hbm, tokens_ref, sems.at[1]),
        pltpu.make_async_copy(taps_hbm, taps_ref, sems.at[2]),
    ]
    for copy in copies:
        copy.start()
    for copy in copies:
        copy.wait()

    now = rounded(dot(tokens_ref[...], w_ref[...]))
    head_ref[...] = now[:HEAD]
    mixed = short_filter_sum(
        taps_ref[:, D:], now, pltpu.roll(now, 1, axis=0), pltpu.roll(now, 2, axis=0)
    )
    product = mixed[:, :D] * mixed[:, D:]
    product_ref[...] = jnp.transpose(product, (1, 0)).astype(jnp.bfloat16)


def project(tokens, w_in, short_filter):
    rows = tokens.shape[0]
    inputs = [
        pltpu.with_memory_space_constraint(a, pltpu.MemorySpace.HBM)
        for a in (tokens, w_in, short_filter)
    ]
    return pl.pallas_call(
        project_kernel,
        out_shape=(
            jax.ShapeDtypeStruct((D, rows), jnp.bfloat16),
            jax.ShapeDtypeStruct((HEAD, 2 * D), jnp.float32),
            jax.ShapeDtypeStruct((D, 2 * D), w_in.dtype),
            jax.ShapeDtypeStruct(short_filter.shape, short_filter.dtype),
        ),
        in_specs=[HBM] * 3,
        out_specs=(VMEM,) * 4,
        scratch_shapes=[pltpu.VMEM(tokens.shape, tokens.dtype), pltpu.SemaphoreType.DMA((3,))],
        compiler_params=pltpu.CompilerParams(vmem_limit_bytes=24 << 20),
        cost_estimate=pl.CostEstimate(
            flops=2 * rows * D * 2 * D, bytes_accessed=2 << 20, transcendentals=0
        ),
        name="project",
    )(*inputs)


def rim_kernel(there_ref, rim_ref, w_ref, taps_ref, head_ref, raw_ref, product_ref):
    before = rounded(dot(rim_ref[...], w_ref[...]))[RIM - HEAD :]
    there = jnp.concatenate([there_ref[0:1], there_ref[0:1]], axis=1)
    before = jnp.where(there > 0.0, before, 0.0)
    both = jnp.concatenate([before, head_ref[...]], axis=0)
    mixed = short_filter_sum(
        taps_ref[:, D:], both, pltpu.roll(both, 1, axis=0), pltpu.roll(both, 2, axis=0)
    )[HEAD:]
    fixed = mixed[:, :D] * mixed[:, D:]
    fixed = jnp.concatenate([fixed, jnp.zeros((LANES - HEAD, D), jnp.float32)], axis=0)
    fixed = jnp.transpose(fixed, (1, 0)).astype(jnp.bfloat16)
    lane = lax.broadcasted_iota(jnp.int32, fixed.shape, 1)
    product_ref[:, LANES:] = raw_ref[:, LANES:]
    product_ref[:, :LANES] = jnp.where(lane < HEAD, fixed, raw_ref[:, :LANES])


def fix_rim(there, rim, w_part, short_filter, head, product):
    return pl.pallas_call(
        rim_kernel,
        out_shape=jax.ShapeDtypeStruct(product.shape, product.dtype),
        in_specs=[VMEM] * 6,
        out_specs=VMEM,
        compiler_params=pltpu.CompilerParams(vmem_limit_bytes=16 << 20),
        cost_estimate=pl.CostEstimate(flops=20_000_000, bytes_accessed=1 << 20, transcendentals=0),
        name="fix_rim",
    )(there, rim, w_part, short_filter, head, product)


def query_kernel(there_ref, tokens_ref, rim_ref, w_ref, taps_ref, query_ref):
    weights = w_ref[:, :D]
    taps = taps_ref[:, :D]
    now = rounded(dot(tokens_ref[...], weights))
    query_ref[...] = short_filter_sum(
        taps, now, pltpu.roll(now, 1, axis=0), pltpu.roll(now, 2, axis=0)
    )
    before = rounded(dot(rim_ref[...], weights))[RIM - HEAD :]
    both = jnp.concatenate([jnp.where(there_ref[0:1] > 0.0, before, 0.0), now[:HEAD]], axis=0)
    query_ref[:HEAD] = short_filter_sum(
        taps, both, pltpu.roll(both, 1, axis=0), pltpu.roll(both, 2, axis=0)
    )[HEAD:]


def make_query(there, tokens, rim, w_in, short_filter):
    rows = tokens.shape[0]
    return pl.pallas_call(
        query_kernel,
        out_shape=jax.ShapeDtypeStruct((rows, D), jnp.float32),
        in_specs=[VMEM] * 5,
        out_specs=VMEM,
        compiler_params=pltpu.CompilerParams(vmem_limit_bytes=16 << 20),
        cost_estimate=pl.CostEstimate(
            flops=2 * rows * D * D, bytes_accessed=1 << 20, transcendentals=0
        ),
        name="make_query",
    )(there, tokens, rim, w_in, short_filter)


def put_rows(load, scratch, chans, tiles, at):
    for tile in range(tiles):
        scratch[pl.ds((at + tile) * chans, chans), :] = load(tile).astype(jnp.float32)


def by_channel(scratch, chans, at, tiles):
    return jnp.concatenate(
        [scratch[pl.ds(at * chans + c, tiles, stride=chans), :] for c in range(chans)], axis=1
    )


def forward(into, cols_in, twist_re, twist_im, data, chans):
    parts = cols_in.shape[0] // (2 * LANES)
    first = dot(into, jnp.concatenate([data, data], axis=0))
    spun = []
    for c in range(chans):
        re = first[:HALF, c * LANES : (c + 1) * LANES]
        im = first[HALF:, c * LANES : (c + 1) * LANES]
        turned = jnp.concatenate(
            [re * twist_re - im * twist_im, re * twist_im + im * twist_re], axis=1
        )
        high = turned.astype(jnp.bfloat16)
        row = [high] * min(parts, 2)
        if parts == 3:
            row.append((turned - high.astype(jnp.float32)).astype(jnp.bfloat16))
        spun.append(jnp.concatenate(row, axis=1) if parts > 1 else high)
    return dot(jnp.concatenate(spun, axis=0), cols_in)


def rows_of(ref):
    per = ref.shape[2] // LANES
    return lambda i: ref[i // per, :, (i % per) * LANES : (i % per + 1) * LANES]


def early_kernel(
    filter_ref, own_ref, gain_ref, into_lo_ref, into_hi_ref, cols_in_ref, twist_ref, spec_ref,
    freq_ref, skip_ref, rows_ref,
):
    chans, taps = filter_ref.shape
    tiles = taps // LANES
    put_rows(lambda i: filter_ref[:, i * LANES : (i + 1) * LANES], rows_ref, chans, tiles, 0)
    gain = jnp.broadcast_to(gain_ref[...], (chans, LANES))
    per = own_ref.shape[2] // LANES
    for tile in range(tiles):
        lanes = slice(tile % per * LANES, (tile % per + 1) * LANES)
        own = own_ref[tile // per, :, lanes].astype(jnp.float32)
        rows_ref[pl.ds((tiles + tile) * chans, chans), :] = own
        skip_ref[tile // per, :, lanes] = gain * own
    twist = twist_ref[0], twist_ref[1]
    data = by_channel(rows_ref, chans, 0, tiles).astype(jnp.bfloat16)
    spec_ref[...] = forward(into_lo_ref[...], cols_in_ref[...], *twist, data, chans)
    data = by_channel(rows_ref, chans, tiles, tiles)
    freq_ref[...] = forward(
        into_hi_ref[...], cols_in_ref[: 4 * LANES], *twist, data.astype(jnp.bfloat16), chans
    )


def early(long_filter, own, gain, into_lo, into_hi, cols_in, twist):
    chans, taps = long_filter.shape
    tiles = taps // LANES
    points = jax.ShapeDtypeStruct((chans * HALF, 2 * LANES), jnp.float32)
    return pl.pallas_call(
        early_kernel,
        out_shape=(points, points, jax.ShapeDtypeStruct(own.shape, jnp.float32)),
        in_specs=[VMEM] * 7,
        out_specs=(VMEM,) * 3,
        scratch_shapes=[pltpu.VMEM((2 * tiles * chans, LANES), jnp.float32)],
        compiler_params=pltpu.CompilerParams(vmem_limit_bytes=24 << 20),
        cost_estimate=pl.CostEstimate(
            flops=800_000_000, bytes_accessed=3 << 20, transcendentals=0
        ),
        name="early",
    )(long_filter, own, gain, into_lo, into_hi, cols_in, twist)


def convolve_kernel(
    there_ref, past_ref, spec_ref, freq_ref, skip_ref, into_lo_ref, cols_in_ref, cols_out_ref,
    back_ref, twist_ref, out_ref, rows_ref,
):
    peers, chans, width = out_ref.shape
    per = width // LANES
    tiles = peers * per
    twist_re = twist_ref[0]
    twist_im = twist_ref[1]
    there = jnp.broadcast_to(there_ref[1:2, :LANES], (chans, LANES)) > 0.0
    load = rows_of(past_ref)
    put_rows(lambda i: jnp.where(there, load(i).astype(jnp.float32), 0.0), rows_ref, chans, tiles, 0)
    past = by_channel(rows_ref, chans, 0, tiles).astype(jnp.bfloat16)
    freq = forward(into_lo_ref[...], cols_in_ref[...], twist_re, twist_im, past, chans) + freq_ref[...]
    spec = spec_ref[...]
    fre, fim = freq[:, :LANES], freq[:, LANES:]
    sre, sim = spec[:, :LANES], spec[:, LANES:]
    prod = jnp.concatenate([fre * sre - fim * sim, fre * sim + fim * sre], axis=1)
    last = dot(prod.astype(jnp.bfloat16), cols_out_ref[...])
    spun = []
    for c in range(chans):
        re = last[c * HALF : (c + 1) * HALF, :LANES]
        im = last[c * HALF : (c + 1) * HALF, LANES:]
        spun.append(
            jnp.concatenate(
                [re * twist_re + im * twist_im, im * twist_re - re * twist_im], axis=0
            ).astype(jnp.bfloat16)
        )
    spun = jnp.concatenate(spun, axis=1)
    result = dot(back_ref[...], jnp.concatenate([spun, spun], axis=0))
    for c in range(chans):
        lanes = slice(c * LANES, (c + 1) * LANES)
        rows_ref[pl.ds(c, tiles, stride=chans), :] = result[:, lanes]
    for tile in range(tiles):
        lanes = slice(tile % per * LANES, (tile % per + 1) * LANES)
        out = rows_ref[pl.ds(tile * chans, chans), :] + skip_ref[tile // per, :, lanes]
        out_ref[tile // per, :, lanes] = out.astype(jnp.bfloat16)


def convolve(there, past, spec, freq, skip, into_lo, cols_in, cols_out, back, twist):
    peers, chans, width = past.shape
    return pl.pallas_call(
        convolve_kernel,
        out_shape=jax.ShapeDtypeStruct(past.shape, jnp.bfloat16),
        in_specs=[VMEM] * 10,
        out_specs=VMEM,
        scratch_shapes=[pltpu.VMEM((peers * chans * width // LANES, LANES), jnp.float32)],
        compiler_params=pltpu.CompilerParams(vmem_limit_bytes=32 << 20),
        cost_estimate=pl.CostEstimate(
            flops=800_000_000, bytes_accessed=4 << 20, transcendentals=0
        ),
        name="convolve",
    )(there, past, spec, freq, skip, into_lo, cols_in, cols_out, back, twist)


def output_kernel(conv_ref, query_ref, w_ref, out_hbm, out_ref, sems):
    rows = query_ref.shape[0] // PIECES
    copies = []
    for piece in range(PIECES):
        at = slice(piece * rows, (piece + 1) * rows)
        conv = jnp.transpose(conv_ref[:, at].astype(jnp.float32), (1, 0))
        gated = (query_ref[at] * conv).astype(jnp.bfloat16)
        out_ref[at] = dot(gated, w_ref[...]).astype(jnp.bfloat16)
        copies.append(pltpu.make_async_copy(out_ref.at[at], out_hbm.at[at], sems.at[piece]))
        copies[-1].start()
    for copy in copies:
        copy.wait()


def project_out(conv, query, w_out):
    rows = query.shape[0]
    return pl.pallas_call(
        output_kernel,
        out_shape=jax.ShapeDtypeStruct((rows, D), jnp.bfloat16),
        in_specs=[VMEM] * 3,
        out_specs=HBM,
        scratch_shapes=[
            pltpu.VMEM((rows, D), jnp.bfloat16), pltpu.SemaphoreType.DMA((PIECES,))
        ],
        compiler_params=pltpu.CompilerParams(vmem_limit_bytes=16 << 20),
        cost_estimate=pl.CostEstimate(
            flops=2 * rows * D * D, bytes_accessed=2 << 20, transcendentals=0
        ),
        name="project_out",
    )(conv, query, w_out)


def rotated(array, axes):
    count = lax.axis_size(axes)
    return lax.ppermute(array, axes, [(i, (i + 1) % count) for i in range(count)])


def per_device(tokens, w_in, short_filter, long_filter, skip_gain, w_out):
    rows = tokens.shape[0]
    peers = lax.axis_size("tok")
    into_lo, into_hi, cols_in, cols_wide, cols_out, back, twist = dft_tables()
    span = lax.axis_index("span")
    there = jnp.stack([span + lax.axis_index("tok") > 0, span > 0]).astype(jnp.float32)
    there = jnp.broadcast_to(there[:, None], (2, D))
    w_in, there = lax.optimization_barrier((w_in, there))
    rim = rotated(tokens[rows - RIM :], ("span", "tok"))
    product, head, w_part, taps = project(tokens, w_in, short_filter)
    head, there, rim = lax.optimization_barrier((head, there, rim))
    product = fix_rim(there, rim, w_part, taps, head, product)
    own = lax.all_to_all(
        product.reshape(peers, D // peers, rows), "tok", split_axis=0, concat_axis=0, tiled=True
    )
    past = rotated(own, "span")
    spec, freq, skip = early(long_filter, own, skip_gain.reshape(-1, 1), into_lo, into_hi, cols_wide, twist)
    query = make_query(there, tokens, rim, w_in, short_filter)
    freq, query = lax.optimization_barrier((freq, query))
    conv = convolve(there, past, spec, freq, skip, into_lo, cols_in, cols_out, back, twist)
    conv = lax.all_to_all(conv, "tok", split_axis=0, concat_axis=0, tiled=True)
    return project_out(conv.reshape(D, rows), query, w_out)


def solution(mesh):
    return jax.shard_map(
        per_device,
        mesh=mesh,
        in_specs=(P(("span", "tok"), None), P(), P(), P("tok", None), P("tok"), P()),
        out_specs=P(("span", "tok"), None),
        check_vma=False,
    )
```
